32 devices in a mesh: tiles: 16 (over z, y, x), grp: 2 (over core).
Axes of the slice: x: 2, y: 2, z: 4, core: 2. Of those that a mesh axis runs over, the one named last changes fastest.
Arguments:
- strips: bfloat16 [64, 256, 4096], P(('tiles', 'grp'))
- edge_colour: int32 [32, 2], P(('tiles', 'grp')), may hold values from 0 to 1, as said below
- patch_offsets: int32 [32, 2, 16, 2], P(('tiles', 'grp')), may hold values from 0 to 3968, as said below
- patch_live: int32 [32, 2], P(('tiles', 'grp')), may hold values from 4 to 16
- node_ids: int32 [32, 2, 16], P(('tiles', 'grp')), may hold values from 0 to 4095
Outputs:
- node_sums: float32 [2, 4096], P(None, ('tiles', 'grp'))
The draws below stay inside these ranges and needn't reach their ends.
Inputs may be any that keep to these rules, and one draw needn't show every extreme that they name: `edge_colour`: for each device its 2 entries name different strips. `patch_offsets`: A device and the device it is paired with in a round have the same offsets in that round. Rows are at most 128.
All inputs are finite; a program needn't handle non-finite values.
Results may differ from the reference program's by a relative error of at most 0.0003.
Values may be sent and summed in bfloat16 or wider, within the bound.
A program may use at most 64 MiB of HBM per device.

```python
import math
import jax
import jax.numpy as jnp
from jax import lax

PATCH = 128
STRIP_R = 256
WIDTH = 4096
ROUNDS = 2
PATCH_DEV = 16
NODES = 4096
N_TILES = 16
N_GRP = 2
DEVICES = 32


def device_flips(key):
    return jax.random.randint(jax.random.fold_in(key, 7), (DEVICES,), 0, 2)


def pair_number(device, round_index):
    tile_index = device // N_GRP
    group_index = device % N_GRP
    pair_bit = jnp.where(round_index == 0, 0, N_TILES.bit_length() - 2)
    side = jnp.right_shift(tile_index, pair_bit) % 2
    lower = tile_index - side * jnp.left_shift(1, pair_bit)
    return ((lower * N_GRP + group_index) * ROUNDS + round_index, side)


def draw_edge_colour(key, part):
    flips = device_flips(key)
    rounds = jnp.arange(ROUNDS, dtype=jnp.int32)
    return jnp.bitwise_xor(rounds[None, :], flips[:, None]).astype(jnp.int32)


def draw_patch_offsets(key, part):

    def single(device, round_index):
        number, side = pair_number(device, round_index)
        pair_key = jax.random.fold_in(key, 5000 + number)
        rows = jax.random.randint(jax.random.fold_in(pair_key, 1), (PATCH_DEV,), 0, STRIP_R - PATCH + 1)
        cols = jax.random.randint(jax.random.fold_in(pair_key, 2), (PATCH_DEV,), 0, WIDTH - PATCH + 1)
        rows = rows.at[0].set(0)
        cols = cols.at[0].set(WIDTH - PATCH)
        return jnp.stack([rows, cols], axis=1)
    devices = jnp.arange(DEVICES, dtype=jnp.int32)
    rounds = jnp.arange(ROUNDS, dtype=jnp.int32)
    table = jax.vmap(lambda device: jax.vmap(lambda rnd: single(device, rnd))(rounds))(devices)
    return table.astype(jnp.int32)


def draw_patch_live(key, part):
    counts = jax.random.randint(jax.random.fold_in(key, 11), (DEVICES, ROUNDS), PATCH_DEV // 4, PATCH_DEV + 1)
    return counts.at[0, 0].set(PATCH_DEV).astype(jnp.int32)


def draw_strips(key, part):
    flips = device_flips(key)
    reach = 3 * PATCH // 8
    block_count = WIDTH // PATCH
    row_positions = jnp.arange(STRIP_R, dtype=jnp.int32)
    col_positions = jnp.arange(WIDTH, dtype=jnp.int32)
    block_of_col = col_positions // PATCH

    def single(index):
        device = index // ROUNDS
        strip_index = index % ROUNDS
        round_index = jnp.bitwise_xor(strip_index, flips[device])
        number, side = pair_number(device, round_index)
        base_key = jax.random.fold_in(key, 100000 + number)
        base = jax.random.normal(base_key, (STRIP_R, WIDTH), jnp.float32)
        row_moves = jax.random.randint(jax.random.fold_in(base_key, 1), (block_count,), -reach, reach + 1)
        col_moves = jax.random.randint(jax.random.fold_in(base_key, 2), (block_count,), -reach, reach + 1)
        row_source = (row_positions[:, None] - side * row_moves[block_of_col][None, :]) % STRIP_R
        col_source = (col_positions[None, :] - side * col_moves[block_of_col][None, :]) % WIDTH
        col_source = jnp.broadcast_to(col_source, (STRIP_R, WIDTH))
        moved = base[row_source, col_source]
        noise = jax.random.normal(jax.random.fold_in(jax.random.fold_in(key, 3), index), (STRIP_R, WIDTH), jnp.float32)
        result = moved + 0.5 * noise
        return result
    return lax.map(single, jnp.arange(DEVICES * ROUNDS, dtype=jnp.int32)).astype(jnp.bfloat16)


def set_ends(drawn, key, least, top_value):
    shape = drawn.shape
    index_at = [jax.random.randint(jax.random.fold_in(key, axis), (), 0, shape[axis]) for axis in range(len(shape))]
    drawn = drawn.at[tuple(index_at)].set(least)
    longest = shape.index(max(shape))
    index_at[longest] = (index_at[longest] + 1) % shape[longest]
    return drawn.at[tuple(index_at)].set(top_value)


def setup_inputs(seed: int = 0) -> dict:
    key_of = jax.random.split(jax.random.key(seed), 6)
    return {
        "strips": draw_strips(jax.random.fold_in(key_of[5], 71), 0),
        "edge_colour": draw_edge_colour(jax.random.fold_in(key_of[5], 71), 0),
        "patch_offsets": draw_patch_offsets(jax.random.fold_in(key_of[5], 71), 0),
        "patch_live": draw_patch_live(jax.random.fold_in(key_of[5], 71), 0),
        "node_ids": set_ends(jax.random.randint(key_of[4], (DEVICES, ROUNDS, PATCH_DEV), 0, NODES), jax.random.fold_in(key_of[4], 1), 0, NODES - 1).astype(jnp.int32),
    }


highest = lax.Precision.HIGHEST

def tables(length):
    indices = jnp.arange(length, dtype=jnp.int32)
    product = indices[:, None] * indices[None, :] % length
    angles = product.astype(jnp.float32) * (2.0 * math.pi / length)
    return (jnp.cos(angles), jnp.sin(angles))

def right_mul(patches, matrix):
    return jnp.einsum('pab,bc->pac', patches, matrix, precision=highest)

def left_mul(matrix, patches):
    return jnp.einsum('ab,pbc->pac', matrix, patches, precision=highest)

def forward(patches, cosine, sine):
    real_half = right_mul(patches, cosine)
    imag_half = -right_mul(patches, sine)
    return (left_mul(cosine, real_half) + left_mul(sine, imag_half), left_mul(cosine, imag_half) - left_mul(sine, real_half))

def displacement(first_set, second_set):
    length = first_set.shape[-1]
    cosine, sine = tables(length)
    first_real, first_imag = forward(first_set, cosine, sine)
    second_real, second_imag = forward(second_set, cosine, sine)
    cross_real = first_real * second_real + first_imag * second_imag
    cross_imag = first_imag * second_real - first_real * second_imag
    magnitude = jnp.sqrt(cross_real * cross_real + cross_imag * cross_imag)
    denominator = magnitude + 0.1 * lax.optimization_barrier(jnp.mean(magnitude, axis=(1, 2), keepdims=True)) + 1e-06
    white_real = cross_real / denominator
    white_imag = cross_imag / denominator
    back_real = left_mul(cosine, white_real) - left_mul(sine, white_imag)
    back_imag = left_mul(cosine, white_imag) + left_mul(sine, white_real)
    surface = (right_mul(back_real, cosine) - right_mul(back_imag, sine)) / float(length * length)
    flattened = surface.reshape(surface.shape[0], length * length)
    centre = lax.optimization_barrier(jnp.mean(flattened, axis=1, keepdims=True))
    spread = jnp.sqrt(lax.optimization_barrier(jnp.mean((flattened - centre) * (flattened - centre), axis=1, keepdims=True)) + 1e-06)
    scores = 2.0 * (flattened - centre) / spread
    weights = jax.nn.softmax(scores, axis=-1).reshape(surface.shape)
    coords = ((jnp.arange(length, dtype=jnp.int32) + length // 2) % length - length // 2).astype(jnp.float32)
    coord_scale = float(length // 8)
    row_shift = lax.optimization_barrier(jnp.sum(weights * coords[None, :, None], axis=(1, 2))) / coord_scale
    col_shift = lax.optimization_barrier(jnp.sum(weights * coords[None, None, :], axis=(1, 2))) / coord_scale
    return jnp.stack([row_shift, col_shift])

def window_stack(strip, offsets):

    def single(corner):
        return lax.dynamic_slice(strip, (corner[0], corner[1]), (PATCH, PATCH))
    return jax.vmap(single)(offsets)

def reference(strips, edge_colour, patch_offsets, patch_live, node_ids):
    stacked = strips.reshape(DEVICES, ROUNDS, STRIP_R, WIDTH)

    def one_device(device):
        tile_index = device // N_GRP
        group_index = device % N_GRP
        first_list = []
        second_list = []
        for round_index in range(ROUNDS):
            pair_bit = 0 if round_index == 0 else N_TILES.bit_length() - 2
            partner = ((tile_index ^ 1 << pair_bit) * N_GRP + group_index).astype(jnp.int32)
            own_strip = stacked[device, edge_colour[device, round_index]]
            other_strip = stacked[partner, edge_colour[partner, round_index]]
            corners = patch_offsets[device, round_index]
            first_list.append(window_stack(own_strip, corners))
            second_list.append(window_stack(other_strip, corners))
        first_set = jnp.concatenate(first_list, axis=0).astype(jnp.float32)
        second_set = jnp.concatenate(second_list, axis=0).astype(jnp.float32)
        shifts = displacement(first_set, second_set)
        slot_index = jnp.arange(PATCH_DEV, dtype=jnp.int32)
        live_mask = (slot_index[None, :] < patch_live[device][:, None]).reshape(ROUNDS * PATCH_DEV)
        return jnp.where(live_mask[None, :], shifts, jnp.zeros_like(shifts))
    values = lax.map(one_device, jnp.arange(DEVICES).astype(jnp.int32))
    values = jnp.transpose(values, (0, 2, 1)).reshape(DEVICES * ROUNDS * PATCH_DEV, 2)
    node_list = node_ids.reshape(DEVICES * ROUNDS * PATCH_DEV)
    summed = jax.ops.segment_sum(values, node_list, num_segments=NODES)
    return jnp.transpose(summed)
```

```python
import functools
import math

import jax
import jax.numpy as jnp
import numpy as np
from jax import lax
from jax.experimental import pallas as pl
from jax.experimental.pallas import tpu as pltpu
from jax.sharding import PartitionSpec as P

PATCH = 128
NODE_DEV = 128
LANES = 128
PACK = 4

F32 = jnp.float32
BF16 = jnp.bfloat16
VMEM = pltpu.MemorySpace.VMEM
SMEM = pltpu.MemorySpace.SMEM


def split_np(x):
    hi = np.asarray(x, np.float32).astype(BF16)
    lo = (np.asarray(x, np.float64) - hi.astype(np.float64)).astype(np.float32).astype(BF16)
    return hi, lo


def tables():
    n = PATCH
    j = np.arange(n)
    angle = 2.0 * math.pi / n * ((j[:, None] * j[None, :]) % n)
    c, s = np.cos(angle), np.sin(angle)
    chi, clo = split_np(np.concatenate([c, s], axis=1))
    col = np.concatenate([chi, clo], axis=0)
    rhi, rlo = split_np(np.block([[c, -s], [s, c]]))
    row = np.concatenate([rhi, rlo, rhi], axis=1)
    ihi, ilo = split_np(np.concatenate([c, s], axis=1))
    inv_row = np.concatenate([ihi, ilo, ihi], axis=1)
    weight = np.where((j == 0) | (j == n // 2), 1.0, 2.0)[:, None]
    packed = np.where(j[:, None] <= n // 2, weight * c, -2.0 * s) / float(n * n)
    vhi, vlo = split_np(packed)
    inv_col = np.concatenate([vhi, vlo, vhi], axis=0)
    return col, row, inv_row, inv_col


def split(x):
    hi = x.astype(BF16)
    return hi, (x - hi.astype(F32)).astype(BF16)


def dot(a, b):
    return jnp.dot(a, b, preferred_element_type=F32)


def extract(half, colour_ref, offset_ref, strip_ref, kept_ref, sent_ref, tmp_ref):
    n = PATCH
    slots = 2 * half
    rnd = pl.program_id(0)
    tile = lax.axis_index("tiles")
    top = lax.axis_size("tiles").bit_length() - 2
    side = jnp.where(rnd == 0, tile % 2, (tile // (1 << top)) % 2)
    height, width = strip_ref.shape[1], strip_ref.shape[2]

    def place(j):
        k = (side * half + j) % slots
        return offset_ref[0, rnd, k, 0], offset_ref[0, rnd, k, 1]

    for j in range(slots):
        row, column = place(j)
        left = jnp.minimum(column // LANES, width // LANES - 2) * LANES
        upper = jnp.minimum(row // 16, (height - n) // 16 - 1) * 16
        block = strip_ref[
            0, pl.ds(pl.multiple_of(upper, 16), n + 16), pl.ds(pl.multiple_of(left, LANES), 2 * LANES)
        ].astype(F32)
        shift = (2 * LANES - (column - left)) % (2 * LANES)
        tmp_ref[j] = pltpu.roll(block, shift, 1)[:, :n]
    for j in range(slots):
        row, column = place(j)
        upper = jnp.minimum(row // 16, (height - n) // 16 - 1) * 16
        window = tmp_ref[j, pl.ds(row - upper, n), :].astype(BF16)
        if j < half:
            kept_ref[0, j] = window
        else:
            sent_ref[0, j - half] = window


def row_place(column, base):
    count = column.shape[0]
    lane = lax.broadcasted_iota(jnp.int32, (count, LANES), 1)
    sub = lax.broadcasted_iota(jnp.int32, (count, LANES), 0)
    return jnp.sum(jnp.where(lane == sub + base, column, 0.0), axis=0, keepdims=True)


def correlate(first, second, col, row, inv_row, inv_col):
    n = PATCH
    count = first.shape[0]
    lane = lax.broadcasted_iota(jnp.int32, (n, n), 1)
    low = lane <= n // 2
    crosses = []
    mag_sums = []
    for p in range(count):
        x = jnp.concatenate([first[p], second[p]], axis=0)
        y = dot(jnp.concatenate([x, x], axis=1), col)
        hi, lo = split(y)

        def stack(v):
            return jnp.concatenate(
                [
                    jnp.concatenate([v[:n, :n], v[n:, :n]], axis=1),
                    jnp.concatenate([v[:n, n:], v[n:, n:]], axis=1),
                ],
                axis=0,
            )

        hi, lo = stack(hi), stack(lo)
        f = dot(row, jnp.concatenate([hi, hi, lo], axis=0))
        r1, r2 = f[:n, :n], f[:n, n:]
        i1, i2 = f[n:, :n], f[n:, n:]
        cross_r = r1 * r2 + i1 * i2
        cross_i = r1 * i2 - i1 * r2
        mag = jnp.sqrt(cross_r * cross_r + cross_i * cross_i)
        crosses.append((cross_r, cross_i, mag))
        mag_sums.append(jnp.sum(mag, axis=0, keepdims=True))
    mean = jnp.sum(jnp.concatenate(mag_sums, axis=0), axis=1, keepdims=True) / float(n * n)
    extra = 0.1 * mean + 1e-06
    surfaces = []
    sums = []
    for p in range(count):
        cross_r, cross_i, mag = crosses[p]
        inverse = 1.0 / (mag + extra[p : p + 1])
        g_r = cross_r * inverse
        g_i = cross_i * inverse
        g = jnp.concatenate([jnp.where(low, g_r, g_i), jnp.where(low, -g_i, g_r)], axis=0)
        hi, lo = split(g)
        b = dot(inv_row, jnp.concatenate([hi, hi, lo], axis=0))
        bhi, blo = split(b)
        surface = dot(jnp.concatenate([bhi, bhi, blo], axis=1), inv_col)
        surfaces.append(surface)
        sums.append(jnp.sum(surface, axis=0, keepdims=True))
    centre = jnp.sum(jnp.concatenate(sums, axis=0), axis=1, keepdims=True) / float(n * n)
    squares = []
    tops = []
    for p in range(count):
        deviation = surfaces[p] - centre[p : p + 1]
        squares.append(jnp.sum(deviation * deviation, axis=0, keepdims=True))
        tops.append(jnp.max(surfaces[p], axis=0, keepdims=True))
    variance = jnp.sum(jnp.concatenate(squares, axis=0), axis=1, keepdims=True) / float(n * n)
    top = jnp.max(jnp.concatenate(tops, axis=0), axis=1, keepdims=True)
    scale = 2.0 / jnp.sqrt(variance + 1e-06)
    sub = lax.broadcasted_iota(jnp.int32, (n, n), 0)
    sub_coord = ((sub + n // 2) % n - n // 2).astype(F32)
    columns = []
    rows = []
    edges = []
    for p in range(count):
        e = jnp.exp((surfaces[p] - top[p : p + 1]) * scale[p : p + 1])
        columns.append(jnp.sum(e, axis=0, keepdims=True))
        rows.append(jnp.sum(e * sub_coord, axis=0, keepdims=True))
        edges.append(e[n // 2 : n // 2 + 1, :])
    columns = jnp.concatenate(columns, axis=0)
    rows = jnp.concatenate(rows, axis=0)
    edges = jnp.concatenate(edges, axis=0)
    lane = lax.broadcasted_iota(jnp.int32, (count, n), 1)
    lane_coord = ((lane + n // 2) % n - n // 2).astype(F32)

    def total(v):
        return jnp.sum(v, axis=1, keepdims=True)

    unit = float(n // 8)
    norm = 1.0 / total(columns)
    row_shift = total(rows) * norm / unit
    col_shift = total(columns * lane_coord) * norm / unit
    row_edge = total(edges) * norm * (float(n) / unit)
    col_edge = total(jnp.where(lane == n // 2, columns, 0.0)) * norm * (float(n) / unit)
    return row_shift, col_shift, -row_shift - row_edge, -col_shift - col_edge


def terms(base, last, first_ref, second_ref, col_ref, row_ref, inv_row_ref, inv_col_ref, *rest):
    count = first_ref.shape[1]
    a, b, c, d = correlate(
        first_ref[0], second_ref[0], col_ref[...], row_ref[...], inv_row_ref[...], inv_col_ref[...]
    )
    row_line = row_place(a, base) + row_place(c, base + count)
    col_line = row_place(b, base) + row_place(d, base + count)
    if last:
        ids_ref, before_ref, out_ref = rest
        row_line = row_line + before_ref[0:1, :]
        col_line = col_line + before_ref[1:2, :]
        id_line = ids_ref[...]
    else:
        (out_ref,) = rest
        id_line = jnp.zeros_like(row_line)
    tile = jnp.concatenate([row_line, col_line, id_line, jnp.zeros((5, LANES), F32)], axis=0)
    if last:
        me = lax.axis_index("tiles") * lax.axis_size("grp") + lax.axis_index("grp")
        tile = pltpu.roll(tile, (me % PACK) * (LANES // PACK), 1)
    out_ref[...] = tile


def gather(devices, tile_ref, out_ref, buf, send_sem, recv_sem):
    groups = lax.axis_size("grp")
    me = lax.axis_index("tiles") * groups + lax.axis_index("grp")
    barrier = pltpu.get_barrier_semaphore()

    def where(i):
        d = lax.rem(me + i, devices)
        return d, (d // groups, d % groups)

    def greet(i, _):
        d, at = where(i)
        pl.semaphore_signal(barrier, inc=1, device_id=at, device_id_type=pl.DeviceIdType.MESH)
        return 0

    lax.fori_loop(1, devices, greet, 0)
    pl.semaphore_wait(barrier, devices - 1)

    def copy(i):
        d, at = where(i)
        return pltpu.make_async_remote_copy(
            src_ref=tile_ref,
            dst_ref=buf.at[i],
            send_sem=send_sem.at[i],
            recv_sem=recv_sem.at[i],
            device_id=at,
            device_id_type=pl.DeviceIdType.MESH,
        )

    def start(i, _):
        copy(i).start()
        return 0

    def finish(i, _):
        copy(i).wait()
        return 0

    lax.fori_loop(1, devices, start, 0)
    buf[0] = tile_ref[...]
    lax.fori_loop(1, devices, finish, 0)
    node = lax.broadcasted_iota(jnp.int32, (NODE_DEV, LANES), 0).astype(F32)
    first_node = (me * NODE_DEV).astype(F32)
    acc = jnp.zeros((8, NODE_DEV), F32)
    for g in range(devices // PACK):
        tile = buf[g * PACK]
        for i in range(1, PACK):
            tile = tile + buf[g * PACK + i]
        onehot = jnp.where(tile[2:3, :] - first_node == node, 1.0, 0.0).astype(BF16)
        hi = tile.astype(BF16)
        rest = tile - hi.astype(F32)
        mid = rest.astype(BF16)
        low = (rest - mid.astype(F32)).astype(BF16)
        stacked = jnp.concatenate([hi, mid, low, jnp.zeros_like(hi)], axis=0)
        part = lax.dot_general(
            stacked, onehot, (((1,), (1,)), ((), ())), preferred_element_type=F32
        )
        acc = acc + (part[0:8] + part[8:16] + part[16:24])
    out_ref[...] = acc[0:2]


def on_device(strips, edge_colour, patch_offsets, patch_live, node_ids):
    rounds = strips.shape[0]
    height, width = strips.shape[1:]
    n = PATCH
    slot_count = patch_offsets.shape[2]
    half = slot_count // 2
    tile_count = lax.axis_size("tiles")
    devices = tile_count * lax.axis_size("grp")
    tile_index = lax.axis_index("tiles")
    col, row, inv_row, inv_col = (jnp.asarray(t) for t in tables())
    window_spec = pl.BlockSpec((1, half, n, n), lambda r, *_: (r, 0, 0, 0))
    kept, sent = pl.pallas_call(
        functools.partial(extract, half),
        out_shape=[jax.ShapeDtypeStruct((rounds, half, n, n), BF16)] * 2,
        grid_spec=pltpu.PrefetchScalarGridSpec(
            num_scalar_prefetch=2,
            grid=(rounds,),
            in_specs=[pl.BlockSpec((1, height, width), lambda r, colour, _: (colour[0, r], 0, 0))],
            out_specs=[window_spec, window_spec],
            scratch_shapes=[pltpu.VMEM((slot_count, n + 16, n), F32)],
        ),
        name="extract",
    )(edge_colour, patch_offsets, strips)

    slot = jnp.arange(slot_count, dtype=jnp.int32)
    ids = jnp.where(slot[None, :] < patch_live[0][:, None], node_ids[0], -1)
    seconds = []
    lines = []
    for r in range(rounds):
        bit = 0 if r == 0 else tile_count.bit_length() - 2
        pairs = [(i, i ^ (1 << bit)) for i in range(tile_count)]
        side = jnp.right_shift(tile_index, bit) % 2
        seconds.append(lax.ppermute(sent[r : r + 1], "tiles", pairs))
        mine = jnp.where(side == 0, ids[r, :half], ids[r, half:])
        other = jnp.where(side == 0, ids[r, half:], ids[r, :half])
        lines += [mine, lax.ppermute(other, "tiles", pairs)]
    id_line = jnp.concatenate(lines).astype(F32)
    id_line = jnp.concatenate([id_line, jnp.full((LANES - id_line.shape[0],), 0.0, F32)])[None, :]

    whole = pl.BlockSpec(memory_space=VMEM)
    tile = None
    for r in range(rounds):
        last = r == rounds - 1
        args = [kept[r : r + 1], seconds[r], col, row, inv_row, inv_col]
        if last:
            args += [id_line, tile]
        tile = pl.pallas_call(
            functools.partial(terms, r * slot_count, last),
            out_shape=jax.ShapeDtypeStruct((8, LANES), F32),
            in_specs=[whole] * len(args),
            out_specs=whole,
            name="terms%d" % r,
            cost_estimate=pl.CostEstimate(
                flops=2 * half * n * n * n * 40, bytes_accessed=4 * half * n * n, transcendentals=half * n * n
            ),
        )(*args)

    return pl.pallas_call(
        functools.partial(gather, devices),
        out_shape=jax.ShapeDtypeStruct((2, NODE_DEV), F32),
        in_specs=[whole],
        out_specs=whole,
        scratch_shapes=[
            pltpu.VMEM((devices, 8, LANES), F32),
            pltpu.SemaphoreType.DMA((devices,)),
            pltpu.SemaphoreType.DMA((devices,)),
        ],
        compiler_params=pltpu.CompilerParams(collective_id=0, has_side_effects=True),
        name="gather",
    )(tile)


def solution(mesh):
    placed = (
        P(("tiles", "grp"), None, None),
        P(("tiles", "grp"), None),
        P(("tiles", "grp"), None, None, None),
        P(("tiles", "grp"), None),
        P(("tiles", "grp"), None, None),
    )
    return jax.shard_map(
        on_device, mesh=mesh, in_specs=placed, out_specs=P(None, ("tiles", "grp")), check_vma=False
    )
```

```python
import functools
import math

import jax
import jax.numpy as jnp
import numpy as np
from jax import lax
from jax.experimental import pallas as pl
from jax.experimental.pallas import tpu as pltpu
from jax.sharding import PartitionSpec as P

PATCH = 128
NODE_DEV = 128
LANES = 128
PACK = 4
GROUP = 4

F32 = jnp.float32
BF16 = jnp.bfloat16
VMEM = pltpu.MemorySpace.VMEM
SMEM = pltpu.MemorySpace.SMEM


def split_np(x):
    hi = np.asarray(x, np.float32).astype(BF16)
    lo = (np.asarray(x, np.float64) - hi.astype(np.float64)).astype(np.float32).astype(BF16)
    return hi, lo


def tables():
    n = PATCH
    j = np.arange(n)
    angle = 2.0 * math.pi / n * ((j[:, None] * j[None, :]) % n)
    c, s = np.cos(angle), np.sin(angle)
    chi, clo = split_np(np.concatenate([c, s], axis=1))
    col = np.concatenate([chi, clo], axis=0)
    rhi, rlo = split_np(np.block([[c, -s], [s, c]]))
    row = np.concatenate([rhi, rlo, rhi], axis=1)
    ihi, ilo = split_np(np.concatenate([c, s], axis=1))
    inv_row = np.concatenate([ihi, ilo, ihi], axis=1)
    weight = np.where((j == 0) | (j == n // 2), 1.0, 2.0)[:, None]
    packed = np.where(j[:, None] <= n // 2, weight * c, -2.0 * s) / float(n * n)
    vhi, vlo = split_np(packed)
    inv_col = np.concatenate([vhi, vlo, vhi], axis=0)
    return col, row, inv_row, inv_col


def split(x):
    hi = x.astype(BF16)
    return hi, (x - hi.astype(F32)).astype(BF16)


def dot(a, b):
    return jnp.dot(a, b, preferred_element_type=F32)


def extract(half, colour_ref, offset_ref, live_ref, ids_ref, strip_ref, kept_ref, sent_ref, line_ref, tmp_ref):
    n = PATCH
    slots = 2 * half
    rnd = pl.program_id(0)
    tile = lax.axis_index("tiles")
    side = jnp.where(rnd == 0, tile % 2, (tile // (lax.axis_size("tiles") // 2)) % 2)
    height, width = strip_ref.shape[1], strip_ref.shape[2]
    rows = []
    for j in range(slots):
        k = (side * half + half + j) % slots
        row, column = offset_ref[0, rnd, 0, k], offset_ref[0, rnd, 1, k]
        left = jnp.minimum(lax.div(column, LANES), width // LANES - 2) * LANES
        upper = jnp.minimum(lax.div(row, 16), (height - n) // 16 - 1) * 16
        block = strip_ref[
            0, pl.ds(pl.multiple_of(upper, 16), n + 16), pl.ds(pl.multiple_of(left, LANES), 2 * LANES)
        ].astype(F32)
        shift = lax.rem(2 * LANES - (column - left), 2 * LANES)
        tmp_ref[j] = pltpu.roll(block, shift, 1)[:, :n]
        rows.append(row - upper)
    for j in range(slots):
        window = tmp_ref[j, pl.ds(rows[j], n), :].astype(BF16)
        ref = sent_ref if j < half else kept_ref
        ref[j % half // GROUP, j % GROUP] = window
    lane = lax.broadcasted_iota(jnp.int32, (1, LANES), 1)
    ids = jnp.zeros((1, LANES), jnp.int32)
    for r in range(live_ref.shape[1]):
        for k in range(slots):
            node = jnp.where(k < live_ref[0, r], ids_ref[0, r, k], -1)
            ids = jnp.where(lane == r * slots + k, node, ids)
    line_ref[...] = ids.astype(F32)


def row_place(column, base):
    count = column.shape[0]
    lane = lax.broadcasted_iota(jnp.int32, (count, LANES), 1)
    sub = lax.broadcasted_iota(jnp.int32, (count, LANES), 0)
    return jnp.sum(jnp.where(lane == sub + base, column, 0.0), axis=0, keepdims=True)


def spectra(windows, col, row):
    n = PATCH
    x = jnp.concatenate(windows, axis=0)
    hi, lo = split(dot(jnp.concatenate([x, x], axis=1), col))

    def stack(v):
        return jnp.concatenate(
            [
                jnp.concatenate([v[:n, :n], v[n:, :n]], axis=1),
                jnp.concatenate([v[:n, n:], v[n:, n:]], axis=1),
            ],
            axis=0,
        )

    hi, lo = stack(hi), stack(lo)
    f = dot(row, jnp.concatenate([hi, hi, lo], axis=0))
    return [(f[:n, :n], f[n:, :n]), (f[:n, n:], f[n:, n:])]


def correlate(first, second, inv_row, inv_col):
    n = PATCH
    count = len(first)
    lane = lax.broadcasted_iota(jnp.int32, (n, n), 1)
    low = lane <= n // 2
    crosses = []
    mag_sums = []
    for (r1, i1), (r2, i2) in zip(first, second):
        cross_r = r1 * r2 + i1 * i2
        cross_i = r1 * i2 - i1 * r2
        mag = jnp.sqrt(cross_r * cross_r + cross_i * cross_i)
        crosses.append((cross_r, cross_i, mag))
        mag_sums.append(jnp.sum(mag, axis=0, keepdims=True))
    mean = jnp.sum(jnp.concatenate(mag_sums, axis=0), axis=1, keepdims=True) / float(n * n)
    extra = 0.1 * mean + 1e-06
    surfaces = []
    sums = []
    for p in range(count):
        cross_r, cross_i, mag = crosses[p]
        inverse = 1.0 / (mag + extra[p : p + 1])
        g_r = cross_r * inverse
        g_i = cross_i * inverse
        g = jnp.concatenate([jnp.where(low, g_r, g_i), jnp.where(low, -g_i, g_r)], axis=0)
        hi, lo = split(g)
        b = dot(inv_row, jnp.concatenate([hi, hi, lo], axis=0))
        bhi, blo = split(b)
        surface = dot(jnp.concatenate([bhi, bhi, blo], axis=1), inv_col)
        surfaces.append(surface)
        sums.append(jnp.sum(surface, axis=0, keepdims=True))
    centre = jnp.sum(jnp.concatenate(sums, axis=0), axis=1, keepdims=True) / float(n * n)
    squares = []
    tops = []
    for p in range(count):
        deviation = surfaces[p] - centre[p : p + 1]
        squares.append(jnp.sum(deviation * deviation, axis=0, keepdims=True))
        tops.append(jnp.max(surfaces[p], axis=0, keepdims=True))
    variance = jnp.sum(jnp.concatenate(squares, axis=0), axis=1, keepdims=True) / float(n * n)
    top = jnp.max(jnp.concatenate(tops, axis=0), axis=1, keepdims=True)
    scale = 2.0 / jnp.sqrt(variance + 1e-06)
    sub = lax.broadcasted_iota(jnp.int32, (n, n), 0)
    sub_coord = ((sub + n // 2) % n - n // 2).astype(F32)
    columns = []
    rows = []
    edges = []
    for p in range(count):
        e = jnp.exp((surfaces[p] - top[p : p + 1]) * scale[p : p + 1])
        columns.append(jnp.sum(e, axis=0, keepdims=True))
        rows.append(jnp.sum(e * sub_coord, axis=0, keepdims=True))
        edges.append(e[n // 2 : n // 2 + 1, :])
    columns = jnp.concatenate(columns, axis=0)
    rows = jnp.concatenate(rows, axis=0)
    edges = jnp.concatenate(edges, axis=0)
    lane = lax.broadcasted_iota(jnp.int32, (count, n), 1)
    lane_coord = ((lane + n // 2) % n - n // 2).astype(F32)

    def total(v):
        return jnp.sum(v, axis=1, keepdims=True)

    unit = float(n // 8)
    norm = 1.0 / total(columns)
    row_shift = total(rows) * norm / unit
    col_shift = total(columns * lane_coord) * norm / unit
    row_edge = total(edges) * norm * (float(n) / unit)
    col_edge = total(jnp.where(lane == n // 2, columns, 0.0)) * norm * (float(n) / unit)
    return row_shift, col_shift, -row_shift - row_edge, -col_shift - col_edge


MESH = pl.DeviceIdType.MESH


def stitch(
    half,
    rounds,
    kept_ref,
    sent,
    line,
    col_ref,
    row_ref,
    inv_row_ref,
    inv_col_ref,
    out_ref,
    kept,
    firsts,
    arrived,
    lines,
    tile_out,
    tiles,
    kept_sem,
    window_send,
    window_recv,
    line_send,
    line_recv,
    tile_send,
    tile_recv,
):
    n = PATCH
    slots = 2 * half
    parts = half // GROUP
    groups = lax.axis_size("grp")
    tile_count = lax.axis_size("tiles")
    devices = tile_count * groups
    tile_index = lax.axis_index("tiles")
    me = tile_index * groups + lax.axis_index("grp")
    strides = [1] + [tile_count // 2] * (rounds - 1)
    sides = [(tile_index // s) % 2 for s in strides]
    partners = [tile_index + s * (1 - 2 * side) for s, side in zip(strides, sides)]

    load = pltpu.make_async_copy(kept_ref, kept, kept_sem)
    load.start()
    barrier = pltpu.get_barrier_semaphore()

    def device(d):
        return (d // groups, d % groups)

    def greet(i, carry):
        pl.semaphore_signal(
            barrier, inc=1, device_id=device((me + i) % devices), device_id_type=MESH
        )
        return carry

    lax.fori_loop(1, devices, greet, 0)

    load.wait()

    def prepare(g, carry):
        for p in range(0, GROUP, 2):
            pair = spectra([kept[g, p], kept[g, p + 1]], col_ref[...], row_ref[...])
            for q in range(2):
                for c in range(2):
                    firsts[g, p + q, c] = pair[q][c]
        return carry

    lax.fori_loop(0, parts, prepare, 0)
    pl.semaphore_wait(barrier, devices - 1)

    def window_copy(r, part):
        g = r * parts + part
        return pltpu.make_async_remote_copy(
            src_ref=sent.at[g],
            dst_ref=arrived.at[g],
            send_sem=window_send.at[g],
            recv_sem=window_recv.at[g],
            device_id=(partners[r], lax.axis_index("grp")),
            device_id_type=MESH,
        )

    def line_copy(r):
        return pltpu.make_async_remote_copy(
            src_ref=line,
            dst_ref=lines.at[r],
            send_sem=line_send.at[r],
            recv_sem=line_recv.at[r],
            device_id=(partners[r], lax.axis_index("grp")),
            device_id_type=MESH,
        )

    for part in range(parts):
        for r in range(rounds):
            window_copy(r, part).start()
    for r in range(rounds):
        line_copy(r).start()

    lax.fori_loop(parts, rounds * parts, prepare, 0)

    def work(g, carry):
        r = g // parts
        pltpu.make_async_remote_copy(
            src_ref=sent.at[g],
            dst_ref=arrived.at[g],
            send_sem=window_send.at[g],
            recv_sem=window_recv.at[g],
            device_id=(partners[0], lax.axis_index("grp")),
            device_id_type=MESH,
        ).wait_recv()
        side = sides[0]
        for i in range(1, rounds):
            side = jnp.where(r == i, sides[i], side)
        seconds = []
        for p in range(0, GROUP, 2):
            seconds += spectra([arrived[g, p], arrived[g, p + 1]], col_ref[...], row_ref[...])
        a, b, c, d = correlate(
            [(firsts[g, p, 0], firsts[g, p, 1]) for p in range(GROUP)],
            seconds,
            inv_row_ref[...],
            inv_col_ref[...],
        )
        base = r * slots + (g % parts) * GROUP
        own = base + side * half
        other = base + (1 - side) * half
        row_line, col_line = carry
        return (
            row_line + row_place(a, own) + row_place(c, other),
            col_line + row_place(b, own) + row_place(d, other),
        )

    zero = jnp.zeros((1, LANES), F32)
    row_line, col_line = lax.fori_loop(0, rounds * parts, work, (zero, zero))

    lane = lax.broadcasted_iota(jnp.int32, (1, LANES), 1)
    ids = line[...]
    id_line = zero
    for r in range(rounds):
        line_copy(r).wait()
        theirs = pltpu.roll(lines[r], jnp.where(sides[r] == 0, half, LANES - half), 1)
        in_round = (lane >= r * slots) & (lane < (r + 1) * slots)
        mine = (lane // half) % 2 == sides[r]
        id_line = id_line + jnp.where(in_round, jnp.where(mine, ids, theirs), 0.0)
    tile = jnp.concatenate([row_line, col_line, id_line, zero], axis=0)
    tile = pltpu.roll(tile, (me % PACK) * (LANES // PACK), 1)
    tile_out[...] = tile
    tiles[me] = tile

    def tile_copy(i, slot):
        return pltpu.make_async_remote_copy(
            src_ref=tile_out,
            dst_ref=tiles.at[slot],
            send_sem=tile_send.at[i],
            recv_sem=tile_recv.at[slot],
            device_id=device((me + i) % devices),
            device_id_type=MESH,
        )

    def start(i, carry):
        tile_copy(i, me).start()
        return carry

    def receive(i, carry):
        tile_copy(i, (me + i) % devices).wait_recv()
        return carry

    def drain(i, carry):
        tile_copy(i, me).wait_send()
        return carry

    lax.fori_loop(1, devices, start, 0)
    for part in range(parts):
        for r in range(rounds):
            window_copy(r, part).wait_send()
    lax.fori_loop(1, devices, receive, 0)

    node = lax.broadcasted_iota(jnp.int32, (NODE_DEV, LANES), 0).astype(F32)
    first_node = (me * NODE_DEV).astype(F32)
    onehots = []
    values = []
    for g in range(devices // PACK):
        tile = tiles[g * PACK]
        for i in range(1, PACK):
            tile = tile + tiles[g * PACK + i]
        onehots.append(jnp.where(tile[2:3] - first_node == node, 1.0, 0.0).astype(BF16))
        hi = tile.astype(BF16).astype(F32)
        rest = tile - hi
        mid = rest.astype(BF16).astype(F32)
        values.append(jnp.concatenate([hi, mid, rest - mid, jnp.zeros_like(hi)], axis=0).astype(BF16))
    result = lax.dot_general(
        jnp.concatenate(values, axis=1),
        jnp.concatenate(onehots, axis=1),
        (((1,), (1,)), ((), ())),
        preferred_element_type=F32,
    )
    out_ref[0:2] = result[0:2]
    out_ref[2:4] = result[4:6] + result[8:10]
    lax.fori_loop(1, devices, drain, 0)


def on_device(strips, edge_colour, patch_offsets, patch_live, node_ids):
    rounds, height, width = strips.shape
    n = PATCH
    slot_count = patch_offsets.shape[2]
    half = slot_count // 2
    parts = half // GROUP
    groups = rounds * parts
    devices = lax.axis_size("tiles") * lax.axis_size("grp")
    whole = pl.BlockSpec(memory_space=VMEM)
    anywhere = pl.BlockSpec(memory_space=pl.ANY)
    sem = pltpu.SemaphoreType.DMA
    windows = (groups, GROUP, n, n)
    window_spec = pl.BlockSpec((parts, GROUP, n, n), lambda r, *_: (r, 0, 0, 0))
    kept, sent, line = pl.pallas_call(
        functools.partial(extract, half),
        out_shape=[jax.ShapeDtypeStruct(windows, BF16)] * 2 + [jax.ShapeDtypeStruct((1, LANES), F32)],
        grid_spec=pltpu.PrefetchScalarGridSpec(
            num_scalar_prefetch=4,
            grid=(rounds,),
            in_specs=[pl.BlockSpec((1, height, width), lambda r, colour, *_: (colour[0, r], 0, 0))],
            out_specs=[window_spec, window_spec, pl.BlockSpec((1, LANES), lambda r, *_: (0, 0))],
            scratch_shapes=[pltpu.VMEM((slot_count, n + 16, n), F32)],
        ),
        name="extract",
    )(edge_colour, jnp.transpose(patch_offsets, (0, 1, 3, 2)), patch_live, node_ids, strips)
    sums = pl.pallas_call(
        functools.partial(stitch, half, rounds),
        out_shape=jax.ShapeDtypeStruct((4, NODE_DEV), F32),
        in_specs=[anywhere] * 2 + [whole] * 5,
        out_specs=whole,
        scratch_shapes=[
            pltpu.VMEM(windows, BF16),
            pltpu.VMEM((groups, GROUP, 2, n, n), F32),
            pltpu.VMEM(windows, BF16),
            pltpu.VMEM((rounds, 1, LANES), F32),
            pltpu.VMEM((4, LANES), F32),
            pltpu.VMEM((devices, 4, LANES), F32),
            sem(()),
            sem((groups,)),
            sem((groups,)),
            sem((rounds,)),
            sem((rounds,)),
            sem((devices,)),
            sem((devices,)),
        ],
        compiler_params=pltpu.CompilerParams(collective_id=0, has_side_effects=True),
        name="stitch",
    )(kept, sent, line, *(jnp.asarray(t) for t in tables()))
    return sums[0:2] + sums[2:4]


def solution(mesh):
    placed = (
        P(("tiles", "grp"), None, None),
        P(("tiles", "grp"), None),
        P(("tiles", "grp"), None, None, None),
        P(("tiles", "grp"), None),
        P(("tiles", "grp"), None, None),
    )
    return jax.shard_map(
        on_device, mesh=mesh, in_specs=placed, out_specs=P(None, ("tiles", "grp")), check_vma=False
    )
```

```python
import functools
import math

import jax
import jax.numpy as jnp
import numpy as np
from jax import lax
from jax.experimental import pallas as pl
from jax.experimental.pallas import tpu as pltpu
from jax.sharding import PartitionSpec as P

PATCH = 128
NODE_DEV = 128
LANES = 128
PACK = 4
GROUP = 4

F32 = jnp.float32
BF16 = jnp.bfloat16
VMEM = pltpu.MemorySpace.VMEM
SMEM = pltpu.MemorySpace.SMEM


def split_np(x):
    hi = np.asarray(x, np.float32).astype(BF16)
    lo = (np.asarray(x, np.float64) - hi.astype(np.float64)).astype(np.float32).astype(BF16)
    return hi, lo


def tables():
    n = PATCH
    j = np.arange(n)
    angle = 2.0 * math.pi / n * ((j[:, None] * j[None, :]) % n)
    c, s = np.cos(angle), np.sin(angle)
    chi, clo = split_np(np.concatenate([c, s], axis=1))
    col = np.concatenate([chi, clo], axis=0)
    rhi, rlo = split_np(np.block([[c, -s], [s, c]]))
    row = np.concatenate([rhi, rlo, rhi], axis=1)
    ihi, ilo = split_np(np.concatenate([c, s], axis=1))
    inv_row = np.concatenate([ihi, ilo, ihi], axis=1)
    weight = np.where((j == 0) | (j == n // 2), 1.0, 2.0)[:, None]
    packed = np.where(j[:, None] <= n // 2, weight * c, -2.0 * s) / float(n * n)
    vhi, vlo = split_np(packed)
    inv_col = np.concatenate([vhi, vlo, vhi], axis=0)
    return col, row, inv_row, inv_col


def split(x):
    hi = x.astype(BF16)
    return hi, (x - hi.astype(F32)).astype(BF16)


def dot(a, b):
    return jnp.dot(a, b, preferred_element_type=F32)


def extract(half, colour_ref, offset_ref, live_ref, ids_ref, strip_ref, kept_ref, sent_ref, line_ref, tmp_ref):
    n = PATCH
    slots = 2 * half
    rnd = pl.program_id(0)
    tile = lax.axis_index("tiles")
    side = jnp.where(rnd == 0, tile % 2, (tile // (lax.axis_size("tiles") // 2)) % 2)
    height, width = strip_ref.shape[1], strip_ref.shape[2]
    rows = []
    for j in range(slots):
        k = (side * half + half + j) % slots
        row, column = offset_ref[0, rnd, 0, k], offset_ref[0, rnd, 1, k]
        left = jnp.minimum(lax.div(column, LANES), width // LANES - 2) * LANES
        upper = jnp.minimum(lax.div(row, 16), (height - n) // 16 - 1) * 16
        block = strip_ref[
            0, pl.ds(pl.multiple_of(upper, 16), n + 16), pl.ds(pl.multiple_of(left, LANES), 2 * LANES)
        ].astype(F32)
        shift = lax.rem(2 * LANES - (column - left), 2 * LANES)
        tmp_ref[j] = pltpu.roll(block, shift, 1)[:, :n]
        rows.append(row - upper)
    for j in range(slots):
        window = tmp_ref[j, pl.ds(rows[j], n), :].astype(BF16)
        ref = sent_ref if j < half else kept_ref
        ref[j % half // GROUP, j % GROUP] = window
    lane = lax.broadcasted_iota(jnp.int32, (1, LANES), 1)
    ids = jnp.zeros((1, LANES), jnp.int32)
    for r in range(live_ref.shape[1]):
        for k in range(slots):
            node = jnp.where(k < live_ref[0, r], ids_ref[0, r, k], -1)
            ids = jnp.where(lane == r * slots + k, node, ids)
    line_ref[...] = ids.astype(F32)


def row_place(column, base):
    count = column.shape[0]
    lane = lax.broadcasted_iota(jnp.int32, (count, LANES), 1)
    sub = lax.broadcasted_iota(jnp.int32, (count, LANES), 0)
    return jnp.sum(jnp.where(lane == sub + base, column, 0.0), axis=0, keepdims=True)


def spectra(windows, col, row):
    n = PATCH
    x = jnp.concatenate(windows, axis=0)
    hi, lo = split(dot(jnp.concatenate([x, x], axis=1), col))

    def stack(v):
        return jnp.concatenate(
            [
                jnp.concatenate([v[:n, :n], v[n:, :n]], axis=1),
                jnp.concatenate([v[:n, n:], v[n:, n:]], axis=1),
            ],
            axis=0,
        )

    hi, lo = stack(hi), stack(lo)
    f = dot(row, jnp.concatenate([hi, hi, lo], axis=0))
    return [(f[:n, :n], f[n:, :n]), (f[:n, n:], f[n:, n:])]


def correlate(first, second, inv_row, inv_col):
    n = PATCH
    count = len(first)
    lane = lax.broadcasted_iota(jnp.int32, (n, n), 1)
    low = lane <= n // 2
    crosses = []
    mag_sums = []
    for (r1, i1), (r2, i2) in zip(first, second):
        cross_r = r1 * r2 + i1 * i2
        cross_i = r1 * i2 - i1 * r2
        mag = jnp.sqrt(cross_r * cross_r + cross_i * cross_i)
        crosses.append((cross_r, cross_i, mag))
        mag_sums.append(jnp.sum(mag, axis=0, keepdims=True))
    mean = jnp.sum(jnp.concatenate(mag_sums, axis=0), axis=1, keepdims=True) / float(n * n)
    extra = 0.1 * mean + 1e-06
    surfaces = []
    sums = []
    for p in range(count):
        cross_r, cross_i, mag = crosses[p]
        inverse = 1.0 / (mag + extra[p : p + 1])
        g_r = cross_r * inverse
        g_i = cross_i * inverse
        g = jnp.concatenate([jnp.where(low, g_r, g_i), jnp.where(low, -g_i, g_r)], axis=0)
        hi, lo = split(g)
        b = dot(inv_row, jnp.concatenate([hi, hi, lo], axis=0))
        bhi, blo = split(b)
        surface = dot(jnp.concatenate([bhi, bhi, blo], axis=1), inv_col)
        surfaces.append(surface)
        sums.append(jnp.sum(surface, axis=0, keepdims=True))
    centre = jnp.sum(jnp.concatenate(sums, axis=0), axis=1, keepdims=True) / float(n * n)
    squares = []
    tops = []
    for p in range(count):
        deviation = surfaces[p] - centre[p : p + 1]
        squares.append(jnp.sum(deviation * deviation, axis=0, keepdims=True))
        tops.append(jnp.max(surfaces[p], axis=0, keepdims=True))
    variance = jnp.sum(jnp.concatenate(squares, axis=0), axis=1, keepdims=True) / float(n * n)
    top = jnp.max(jnp.concatenate(tops, axis=0), axis=1, keepdims=True)
    scale = 2.0 / jnp.sqrt(variance + 1e-06)
    sub = lax.broadcasted_iota(jnp.int32, (n, n), 0)
    sub_coord = ((sub + n // 2) % n - n // 2).astype(F32)
    columns = []
    rows = []
    edges = []
    for p in range(count):
        e = jnp.exp((surfaces[p] - top[p : p + 1]) * scale[p : p + 1])
        columns.append(jnp.sum(e, axis=0, keepdims=True))
        rows.append(jnp.sum(e * sub_coord, axis=0, keepdims=True))
        edges.append(e[n // 2 : n // 2 + 1, :])
    columns = jnp.concatenate(columns, axis=0)
    rows = jnp.concatenate(rows, axis=0)
    edges = jnp.concatenate(edges, axis=0)
    lane = lax.broadcasted_iota(jnp.int32, (count, n), 1)
    lane_coord = ((lane + n // 2) % n - n // 2).astype(F32)

    def total(v):
        return jnp.sum(v, axis=1, keepdims=True)

    unit = float(n // 8)
    norm = 1.0 / total(columns)
    row_shift = total(rows) * norm / unit
    col_shift = total(columns * lane_coord) * norm / unit
    row_edge = total(edges) * norm * (float(n) / unit)
    col_edge = total(jnp.where(lane == n // 2, columns, 0.0)) * norm * (float(n) / unit)
    return row_shift, col_shift, -row_shift - row_edge, -col_shift - col_edge


MESH = pl.DeviceIdType.MESH


def stitch(
    half,
    rounds,
    kept_ref,
    sent,
    line,
    col_ref,
    row_ref,
    inv_row_ref,
    inv_col_ref,
    out_ref,
    kept,
    firsts,
    arrived,
    lines,
    tile_out,
    tiles,
    kept_sem,
    window_send,
    window_recv,
    line_send,
    line_recv,
    tile_send,
    tile_recv,
    hello,
):
    n = PATCH
    slots = 2 * half
    parts = half // GROUP
    groups = lax.axis_size("grp")
    tile_count = lax.axis_size("tiles")
    devices = tile_count * groups
    tile_index = lax.axis_index("tiles")
    me = tile_index * groups + lax.axis_index("grp")
    strides = [1] + [tile_count // 2] * (rounds - 1)
    sides = [(tile_index // s) % 2 for s in strides]
    partners = [tile_index + s * (1 - 2 * side) for s, side in zip(strides, sides)]

    load = pltpu.make_async_copy(kept_ref, kept, kept_sem)
    load.start()
    barrier = pltpu.get_barrier_semaphore()

    def device(d):
        return (d // groups, d % groups)

    neighbours = []
    stride = 1
    while stride < tile_count:
        bit = (tile_index // stride) % 2
        neighbours.append((tile_index + stride * (1 - 2 * bit), lax.axis_index("grp")))
        stride *= 2
    stride = 1
    while stride < groups:
        bit = (lax.axis_index("grp") // stride) % 2
        neighbours.append((tile_index, lax.axis_index("grp") + stride * (1 - 2 * bit)))
        stride *= 2
    stages = len(neighbours)
    for at in neighbours:
        pl.semaphore_signal(barrier, inc=1, device_id=at, device_id_type=MESH)

    def neighbour(stage):
        tile, group = neighbours[0]
        for i in range(1, stages):
            tile = jnp.where(stage == i, neighbours[i][0], tile)
            group = jnp.where(stage == i, neighbours[i][1], group)
        return tile, group

    def hail(stage):
        pl.semaphore_signal(
            hello.at[stage], inc=1, device_id=neighbour(stage), device_id_type=MESH
        )

    load.wait()

    def prepare(g, carry):
        for p in range(0, GROUP, 2):
            pair = spectra([kept[g, p], kept[g, p + 1]], col_ref[...], row_ref[...])
            for q in range(2):
                for c in range(2):
                    firsts[g, p + q, c] = pair[q][c]
        return carry

    lax.fori_loop(0, 1, prepare, 0)
    pl.semaphore_wait(barrier, stages)

    def window_copy(r, part):
        g = r * parts + part
        return pltpu.make_async_remote_copy(
            src_ref=sent.at[g],
            dst_ref=arrived.at[g],
            send_sem=window_send.at[g],
            recv_sem=window_recv.at[g],
            device_id=(partners[r], lax.axis_index("grp")),
            device_id_type=MESH,
        )

    def line_copy(r):
        return pltpu.make_async_remote_copy(
            src_ref=line,
            dst_ref=lines.at[r],
            send_sem=line_send.at[r],
            recv_sem=line_recv.at[r],
            device_id=(partners[r], lax.axis_index("grp")),
            device_id_type=MESH,
        )

    for part in range(parts):
        for r in range(rounds):
            window_copy(r, part).start()
    for r in range(rounds):
        line_copy(r).start()

    early = stages - rounds * parts
    for i in range(early):
        hail(i)
        if i == early - 1:
            lax.fori_loop(1, rounds * parts, prepare, 0)
        pl.semaphore_wait(hello.at[i], 1)

    def work(g, carry):
        r = g // parts
        hail(early + g)
        pltpu.make_async_remote_copy(
            src_ref=sent.at[g],
            dst_ref=arrived.at[g],
            send_sem=window_send.at[g],
            recv_sem=window_recv.at[g],
            device_id=(partners[0], lax.axis_index("grp")),
            device_id_type=MESH,
        ).wait_recv()
        side = sides[0]
        for i in range(1, rounds):
            side = jnp.where(r == i, sides[i], side)
        seconds = []
        for p in range(0, GROUP, 2):
            seconds += spectra([arrived[g, p], arrived[g, p + 1]], col_ref[...], row_ref[...])
        a, b, c, d = correlate(
            [(firsts[g, p, 0], firsts[g, p, 1]) for p in range(GROUP)],
            seconds,
            inv_row_ref[...],
            inv_col_ref[...],
        )
        base = r * slots + (g % parts) * GROUP
        own = base + side * half
        other = base + (1 - side) * half
        row_line, col_line = carry
        pl.semaphore_wait(hello.at[early + g], 1)
        return (
            row_line + row_place(a, own) + row_place(c, other),
            col_line + row_place(b, own) + row_place(d, other),
        )

    zero = jnp.zeros((1, LANES), F32)
    row_line, col_line = lax.fori_loop(0, rounds * parts, work, (zero, zero))

    lane = lax.broadcasted_iota(jnp.int32, (1, LANES), 1)
    ids = line[...]
    id_line = zero
    for r in range(rounds):
        line_copy(r).wait()
        theirs = pltpu.roll(lines[r], jnp.where(sides[r] == 0, half, LANES - half), 1)
        in_round = (lane >= r * slots) & (lane < (r + 1) * slots)
        mine = (lane // half) % 2 == sides[r]
        id_line = id_line + jnp.where(in_round, jnp.where(mine, ids, theirs), 0.0)
    tile = jnp.concatenate([row_line, col_line, id_line, zero], axis=0)
    tile = pltpu.roll(tile, (me % PACK) * (LANES // PACK), 1)
    tile_out[...] = tile
    tiles[me] = tile

    def tile_copy(i, slot):
        return pltpu.make_async_remote_copy(
            src_ref=tile_out,
            dst_ref=tiles.at[slot],
            send_sem=tile_send.at[i],
            recv_sem=tile_recv.at[slot],
            device_id=device((me + i) % devices),
            device_id_type=MESH,
        )

    def start(i, carry):
        tile_copy(i, me).start()
        return carry

    def receive(i, carry):
        tile_copy(i, (me + i) % devices).wait_recv()
        return carry

    def drain(i, carry):
        tile_copy(i, me).wait_send()
        return carry

    lax.fori_loop(1, devices, start, 0)
    for part in range(parts):
        for r in range(rounds):
            window_copy(r, part).wait_send()
    lax.fori_loop(1, devices, receive, 0)

    node = lax.broadcasted_iota(jnp.int32, (NODE_DEV, LANES), 0).astype(F32)
    first_node = (me * NODE_DEV).astype(F32)
    onehots = []
    values = []
    for g in range(devices // PACK):
        tile = tiles[g * PACK]
        for i in range(1, PACK):
            tile = tile + tiles[g * PACK + i]
        onehots.append(jnp.where(tile[2:3] - first_node == node, 1.0, 0.0).astype(BF16))
        hi = tile.astype(BF16).astype(F32)
        rest = tile - hi
        mid = rest.astype(BF16).astype(F32)
        values.append(jnp.concatenate([hi, mid, rest - mid, jnp.zeros_like(hi)], axis=0).astype(BF16))
    result = lax.dot_general(
        jnp.concatenate(values, axis=1),
        jnp.concatenate(onehots, axis=1),
        (((1,), (1,)), ((), ())),
        preferred_element_type=F32,
    )
    out_ref[0:2] = result[0:2]
    out_ref[2:4] = result[4:6] + result[8:10]
    lax.fori_loop(1, devices, drain, 0)


def on_device(strips, edge_colour, patch_offsets, patch_live, node_ids):
    rounds, height, width = strips.shape
    n = PATCH
    slot_count = patch_offsets.shape[2]
    half = slot_count // 2
    parts = half // GROUP
    groups = rounds * parts
    devices = lax.axis_size("tiles") * lax.axis_size("grp")
    whole = pl.BlockSpec(memory_space=VMEM)
    anywhere = pl.BlockSpec(memory_space=pl.ANY)
    sem = pltpu.SemaphoreType.DMA
    windows = (groups, GROUP, n, n)
    window_spec = pl.BlockSpec((parts, GROUP, n, n), lambda r, *_: (r, 0, 0, 0))
    kept, sent, line = pl.pallas_call(
        functools.partial(extract, half),
        out_shape=[jax.ShapeDtypeStruct(windows, BF16)] * 2 + [jax.ShapeDtypeStruct((1, LANES), F32)],
        grid_spec=pltpu.PrefetchScalarGridSpec(
            num_scalar_prefetch=4,
            grid=(rounds,),
            in_specs=[pl.BlockSpec((1, height, width), lambda r, colour, *_: (colour[0, r], 0, 0))],
            out_specs=[window_spec, window_spec, pl.BlockSpec((1, LANES), lambda r, *_: (0, 0))],
            scratch_shapes=[pltpu.VMEM((slot_count, n + 16, n), F32)],
        ),
        name="extract",
    )(edge_colour, jnp.transpose(patch_offsets, (0, 1, 3, 2)), patch_live, node_ids, strips)
    sums = pl.pallas_call(
        functools.partial(stitch, half, rounds),
        out_shape=jax.ShapeDtypeStruct((4, NODE_DEV), F32),
        in_specs=[anywhere] * 2 + [whole] * 5,
        out_specs=whole,
        scratch_shapes=[
            pltpu.VMEM(windows, BF16),
            pltpu.VMEM((groups, GROUP, 2, n, n), F32),
            pltpu.VMEM(windows, BF16),
            pltpu.VMEM((rounds, 1, LANES), F32),
            pltpu.VMEM((4, LANES), F32),
            pltpu.VMEM((devices, 4, LANES), F32),
            sem(()),
            sem((groups,)),
            sem((groups,)),
            sem((rounds,)),
            sem((rounds,)),
            sem((devices,)),
            sem((devices,)),
            pltpu.SemaphoreType.REGULAR((devices.bit_length() - 1,)),
        ],
        compiler_params=pltpu.CompilerParams(collective_id=0, has_side_effects=True),
        name="stitch",
    )(kept, sent, line, *(jnp.asarray(t) for t in tables()))
    return sums[0:2] + sums[2:4]


def solution(mesh):
    placed = (
        P(("tiles", "grp"), None, None),
        P(("tiles", "grp"), None),
        P(("tiles", "grp"), None, None, None),
        P(("tiles", "grp"), None),
        P(("tiles", "grp"), None, None),
    )
    return jax.shard_map(
        on_device, mesh=mesh, in_specs=placed, out_specs=P(None, ("tiles", "grp")), check_vma=False
    )
```

```python
import functools
import math

import jax
import jax.numpy as jnp
import numpy as np
from jax import lax
from jax.experimental import pallas as pl
from jax.experimental.pallas import tpu as pltpu
from jax.sharding import PartitionSpec as P

PATCH = 128
NODE_DEV = 128
LANES = 128
PACK = 4
GROUP = 4

F32 = jnp.float32
BF16 = jnp.bfloat16
VMEM = pltpu.MemorySpace.VMEM
SMEM = pltpu.MemorySpace.SMEM


def split_np(x):
    hi = np.asarray(x, np.float32).astype(BF16)
    lo = (np.asarray(x, np.float64) - hi.astype(np.float64)).astype(np.float32).astype(BF16)
    return hi, lo


def tables():
    n = PATCH
    j = np.arange(n)
    angle = 2.0 * math.pi / n * ((j[:, None] * j[None, :]) % n)
    c, s = np.cos(angle), np.sin(angle)
    chi, clo = split_np(np.concatenate([c, s], axis=1))
    col = np.concatenate([chi, clo], axis=0)
    rhi, rlo = split_np(np.block([[c, -s], [s, c]]))
    row = np.concatenate([rhi, rlo, rhi], axis=1)
    ihi, ilo = split_np(np.concatenate([c, s], axis=1))
    inv_row = np.concatenate([ihi, ilo, ihi], axis=1)
    weight = np.where((j == 0) | (j == n // 2), 1.0, 2.0)[:, None]
    packed = np.where(j[:, None] <= n // 2, weight * c, -2.0 * s) / float(n * n)
    vhi, vlo = split_np(packed)
    inv_col = np.concatenate([vhi, vlo, vhi], axis=0)
    return col, row, inv_row, inv_col


def split(x):
    hi = x.astype(BF16)
    return hi, (x - hi.astype(F32)).astype(BF16)


def dot(a, b):
    return jnp.dot(a, b, preferred_element_type=F32)


def extract(half, colour_ref, offset_ref, live_ref, ids_ref, strip_ref, kept_ref, sent_ref, line_ref, tmp_ref):
    n = PATCH
    slots = 2 * half
    rnd = pl.program_id(0)
    tile = lax.axis_index("tiles")
    side = jnp.where(rnd == 0, tile % 2, (tile // (lax.axis_size("tiles") // 2)) % 2)
    height, width = strip_ref.shape[1], strip_ref.shape[2]
    rows = []
    for j in range(slots):
        k = (side * half + half + j) % slots
        row, column = offset_ref[0, rnd, 0, k], offset_ref[0, rnd, 1, k]
        left = jnp.minimum(lax.div(column, LANES), width // LANES - 2) * LANES
        upper = jnp.minimum(lax.div(row, 16), (height - n) // 16 - 1) * 16
        block = strip_ref[
            0, pl.ds(pl.multiple_of(upper, 16), n + 16), pl.ds(pl.multiple_of(left, LANES), 2 * LANES)
        ].astype(F32)
        shift = lax.rem(2 * LANES - (column - left), 2 * LANES)
        tmp_ref[j] = pltpu.roll(block, shift, 1)[:, :n]
        rows.append(row - upper)
    for j in range(slots):
        window = tmp_ref[j, pl.ds(rows[j], n), :].astype(BF16)
        ref = sent_ref if j < half else kept_ref
        ref[j % half // GROUP, j % GROUP] = window
    lane = lax.broadcasted_iota(jnp.int32, (1, LANES), 1)
    ids = jnp.zeros((1, LANES), jnp.int32)
    for r in range(live_ref.shape[1]):
        for k in range(slots):
            node = jnp.where(k < live_ref[0, r], ids_ref[0, r, k], -1)
            ids = jnp.where(lane == r * slots + k, node, ids)
    line_ref[...] = ids.astype(F32)


def row_place(column, base):
    count = column.shape[0]
    lane = lax.broadcasted_iota(jnp.int32, (count, LANES), 1)
    sub = lax.broadcasted_iota(jnp.int32, (count, LANES), 0)
    return jnp.sum(jnp.where(lane == sub + base, column, 0.0), axis=0, keepdims=True)


def spectra(windows, col, row):
    n = PATCH
    x = jnp.concatenate(windows, axis=0)
    hi, lo = split(dot(jnp.concatenate([x, x], axis=1), col))

    def stack(v):
        return jnp.concatenate(
            [
                jnp.concatenate([v[:n, :n], v[n:, :n]], axis=1),
                jnp.concatenate([v[:n, n:], v[n:, n:]], axis=1),
            ],
            axis=0,
        )

    hi, lo = stack(hi), stack(lo)
    f = dot(row, jnp.concatenate([hi, hi, lo], axis=0))
    return [(f[:n, :n], f[n:, :n]), (f[:n, n:], f[n:, n:])]


def correlate(first, second, inv_row, inv_col):
    n = PATCH
    count = len(first)
    lane = lax.broadcasted_iota(jnp.int32, (n, n), 1)
    low = lane <= n // 2
    crosses = []
    mag_sums = []
    for (r1, i1), (r2, i2) in zip(first, second):
        cross_r = r1 * r2 + i1 * i2
        cross_i = r1 * i2 - i1 * r2
        mag = jnp.sqrt(cross_r * cross_r + cross_i * cross_i)
        crosses.append((cross_r, cross_i, mag))
        mag_sums.append(jnp.sum(mag, axis=0, keepdims=True))
    mean = jnp.sum(jnp.concatenate(mag_sums, axis=0), axis=1, keepdims=True) / float(n * n)
    extra = 0.1 * mean + 1e-06
    surfaces = []
    packed = []
    sums = []
    for p in range(count):
        cross_r, cross_i, mag = crosses[p]
        inverse = 1.0 / (mag + extra[p : p + 1])
        g_r = cross_r * inverse
        g_i = cross_i * inverse
        packed.append(
            split(jnp.concatenate([jnp.where(low, g_r, g_i), jnp.where(low, -g_i, g_r)], axis=0))
        )
    surfaces_wide = []
    for p in range(0, count, 2):
        hi = jnp.concatenate([packed[p][0], packed[p + 1][0]], axis=1)
        lo = jnp.concatenate([packed[p][1], packed[p + 1][1]], axis=1)
        b = dot(inv_row, jnp.concatenate([hi, hi, lo], axis=0))
        bhi, blo = split(jnp.concatenate([b[:, :n], b[:, n:]], axis=0))
        wide = dot(jnp.concatenate([bhi, bhi, blo], axis=1), inv_col)
        surfaces_wide += [wide[:n], wide[n:]]
    for surface in surfaces_wide:
        surfaces.append(surface)
        sums.append(jnp.sum(surface, axis=0, keepdims=True))
    centre = jnp.sum(jnp.concatenate(sums, axis=0), axis=1, keepdims=True) / float(n * n)
    squares = []
    tops = []
    for p in range(count):
        deviation = surfaces[p] - centre[p : p + 1]
        squares.append(jnp.sum(deviation * deviation, axis=0, keepdims=True))
        tops.append(jnp.max(surfaces[p], axis=0, keepdims=True))
    variance = jnp.sum(jnp.concatenate(squares, axis=0), axis=1, keepdims=True) / float(n * n)
    top = jnp.max(jnp.concatenate(tops, axis=0), axis=1, keepdims=True)
    scale = 2.0 / jnp.sqrt(variance + 1e-06)
    sub = lax.broadcasted_iota(jnp.int32, (n, n), 0)
    sub_coord = ((sub + n // 2) % n - n // 2).astype(F32)
    columns = []
    rows = []
    edges = []
    for p in range(count):
        e = jnp.exp((surfaces[p] - top[p : p + 1]) * scale[p : p + 1])
        columns.append(jnp.sum(e, axis=0, keepdims=True))
        rows.append(jnp.sum(e * sub_coord, axis=0, keepdims=True))
        edges.append(e[n // 2 : n // 2 + 1, :])
    columns = jnp.concatenate(columns, axis=0)
    rows = jnp.concatenate(rows, axis=0)
    edges = jnp.concatenate(edges, axis=0)
    lane = lax.broadcasted_iota(jnp.int32, (count, n), 1)
    lane_coord = ((lane + n // 2) % n - n // 2).astype(F32)

    def total(v):
        return jnp.sum(v, axis=1, keepdims=True)

    unit = float(n // 8)
    norm = 1.0 / total(columns)
    row_shift = total(rows) * norm / unit
    col_shift = total(columns * lane_coord) * norm / unit
    row_edge = total(edges) * norm * (float(n) / unit)
    col_edge = total(jnp.where(lane == n // 2, columns, 0.0)) * norm * (float(n) / unit)
    return row_shift, col_shift, -row_shift - row_edge, -col_shift - col_edge


MESH = pl.DeviceIdType.MESH


def stitch(
    half,
    rounds,
    kept_ref,
    sent,
    line,
    col_ref,
    row_ref,
    inv_row_ref,
    inv_col_ref,
    out_ref,
    kept,
    firsts,
    arrived,
    lines,
    tile_out,
    tiles,
    kept_sem,
    window_send,
    window_recv,
    line_send,
    line_recv,
    tile_send,
    tile_recv,
    hello,
):
    n = PATCH
    slots = 2 * half
    parts = half // GROUP
    groups = lax.axis_size("grp")
    tile_count = lax.axis_size("tiles")
    devices = tile_count * groups
    tile_index = lax.axis_index("tiles")
    me = tile_index * groups + lax.axis_index("grp")
    strides = [1] + [tile_count // 2] * (rounds - 1)
    sides = [(tile_index // s) % 2 for s in strides]
    partners = [tile_index + s * (1 - 2 * side) for s, side in zip(strides, sides)]

    load = pltpu.make_async_copy(kept_ref, kept, kept_sem)
    load.start()
    barrier = pltpu.get_barrier_semaphore()

    def device(d):
        return (d // groups, d % groups)

    neighbours = []
    stride = 1
    while stride < tile_count:
        bit = (tile_index // stride) % 2
        neighbours.append((tile_index + stride * (1 - 2 * bit), lax.axis_index("grp")))
        stride *= 2
    stride = 1
    while stride < groups:
        bit = (lax.axis_index("grp") // stride) % 2
        neighbours.append((tile_index, lax.axis_index("grp") + stride * (1 - 2 * bit)))
        stride *= 2
    stages = len(neighbours)
    for at in neighbours:
        pl.semaphore_signal(barrier, inc=1, device_id=at, device_id_type=MESH)

    def neighbour(stage):
        tile, group = neighbours[0]
        for i in range(1, stages):
            tile = jnp.where(stage == i, neighbours[i][0], tile)
            group = jnp.where(stage == i, neighbours[i][1], group)
        return tile, group

    def hail(stage):
        pl.semaphore_signal(
            hello.at[stage], inc=1, device_id=neighbour(stage), device_id_type=MESH
        )

    load.wait()

    def prepare(g, carry):
        for p in range(0, GROUP, 2):
            pair = spectra([kept[g, p], kept[g, p + 1]], col_ref[...], row_ref[...])
            for q in range(2):
                for c in range(2):
                    firsts[g, p + q, c] = pair[q][c]
        return carry

    lax.fori_loop(0, 1, prepare, 0)
    pl.semaphore_wait(barrier, stages)

    def window_copy(r, part):
        g = r * parts + part
        return pltpu.make_async_remote_copy(
            src_ref=sent.at[g],
            dst_ref=arrived.at[g],
            send_sem=window_send.at[g],
            recv_sem=window_recv.at[g],
            device_id=(partners[r], lax.axis_index("grp")),
            device_id_type=MESH,
        )

    def line_copy(r):
        return pltpu.make_async_remote_copy(
            src_ref=line,
            dst_ref=lines.at[r],
            send_sem=line_send.at[r],
            recv_sem=line_recv.at[r],
            device_id=(partners[r], lax.axis_index("grp")),
            device_id_type=MESH,
        )

    for part in range(parts):
        for r in range(rounds):
            window_copy(r, part).start()
    for r in range(rounds):
        line_copy(r).start()

    early = stages - rounds * parts
    for i in range(early):
        hail(i)
        if i == early - 1:
            lax.fori_loop(1, rounds * parts, prepare, 0)
        pl.semaphore_wait(hello.at[i], 1)

    def work(g, carry):
        r = g // parts
        hail(early + g)
        pltpu.make_async_remote_copy(
            src_ref=sent.at[g],
            dst_ref=arrived.at[g],
            send_sem=window_send.at[g],
            recv_sem=window_recv.at[g],
            device_id=(partners[0], lax.axis_index("grp")),
            device_id_type=MESH,
        ).wait_recv()
        side = sides[0]
        for i in range(1, rounds):
            side = jnp.where(r == i, sides[i], side)
        seconds = []
        for p in range(0, GROUP, 2):
            seconds += spectra([arrived[g, p], arrived[g, p + 1]], col_ref[...], row_ref[...])
        a, b, c, d = correlate(
            [(firsts[g, p, 0], firsts[g, p, 1]) for p in range(GROUP)],
            seconds,
            inv_row_ref[...],
            inv_col_ref[...],
        )
        base = r * slots + (g % parts) * GROUP
        own = base + side * half
        other = base + (1 - side) * half
        row_line, col_line = carry
        pl.semaphore_wait(hello.at[early + g], 1)
        return (
            row_line + row_place(a, own) + row_place(c, other),
            col_line + row_place(b, own) + row_place(d, other),
        )

    zero = jnp.zeros((1, LANES), F32)
    row_line, col_line = lax.fori_loop(0, rounds * parts, work, (zero, zero))

    lane = lax.broadcasted_iota(jnp.int32, (1, LANES), 1)
    ids = line[...]
    id_line = zero
    for r in range(rounds):
        line_copy(r).wait()
        theirs = pltpu.roll(lines[r], jnp.where(sides[r] == 0, half, LANES - half), 1)
        in_round = (lane >= r * slots) & (lane < (r + 1) * slots)
        mine = (lane // half) % 2 == sides[r]
        id_line = id_line + jnp.where(in_round, jnp.where(mine, ids, theirs), 0.0)
    tile = jnp.concatenate([row_line, col_line, id_line, zero], axis=0)
    tile = pltpu.roll(tile, (me % PACK) * (LANES // PACK), 1)
    tile_out[...] = tile
    tiles[me] = tile

    def tile_copy(i, slot):
        return pltpu.make_async_remote_copy(
            src_ref=tile_out,
            dst_ref=tiles.at[slot],
            send_sem=tile_send.at[i],
            recv_sem=tile_recv.at[slot],
            device_id=device((me + i) % devices),
            device_id_type=MESH,
        )

    def start(i, carry):
        tile_copy(i, me).start()
        return carry

    def receive(i, carry):
        tile_copy(i, (me + i) % devices).wait_recv()
        return carry

    def drain(i, carry):
        tile_copy(i, me).wait_send()
        return carry

    lax.fori_loop(1, devices, start, 0)
    for part in range(parts):
        for r in range(rounds):
            window_copy(r, part).wait_send()
    lax.fori_loop(1, devices, receive, 0)

    node = lax.broadcasted_iota(jnp.int32, (NODE_DEV, LANES), 0).astype(F32)
    first_node = (me * NODE_DEV).astype(F32)
    onehots = []
    values = []
    for g in range(devices // PACK):
        tile = tiles[g * PACK]
        for i in range(1, PACK):
            tile = tile + tiles[g * PACK + i]
        onehots.append(jnp.where(tile[2:3] - first_node == node, 1.0, 0.0).astype(BF16))
        hi = tile.astype(BF16).astype(F32)
        rest = tile - hi
        mid = rest.astype(BF16).astype(F32)
        values.append(jnp.concatenate([hi, mid, rest - mid, jnp.zeros_like(hi)], axis=0).astype(BF16))
    result = lax.dot_general(
        jnp.concatenate(values, axis=1),
        jnp.concatenate(onehots, axis=1),
        (((1,), (1,)), ((), ())),
        preferred_element_type=F32,
    )
    out_ref[0:2] = result[0:2]
    out_ref[2:4] = result[4:6] + result[8:10]
    lax.fori_loop(1, devices, drain, 0)


def on_device(strips, edge_colour, patch_offsets, patch_live, node_ids):
    rounds, height, width = strips.shape
    n = PATCH
    slot_count = patch_offsets.shape[2]
    half = slot_count // 2
    parts = half // GROUP
    groups = rounds * parts
    devices = lax.axis_size("tiles") * lax.axis_size("grp")
    whole = pl.BlockSpec(memory_space=VMEM)
    anywhere = pl.BlockSpec(memory_space=pl.ANY)
    sem = pltpu.SemaphoreType.DMA
    windows = (groups, GROUP, n, n)
    window_spec = pl.BlockSpec((parts, GROUP, n, n), lambda r, *_: (r, 0, 0, 0))
    kept, sent, line = pl.pallas_call(
        functools.partial(extract, half),
        out_shape=[jax.ShapeDtypeStruct(windows, BF16)] * 2 + [jax.ShapeDtypeStruct((1, LANES), F32)],
        grid_spec=pltpu.PrefetchScalarGridSpec(
            num_scalar_prefetch=4,
            grid=(rounds,),
            in_specs=[pl.BlockSpec((1, height, width), lambda r, colour, *_: (colour[0, r], 0, 0))],
            out_specs=[window_spec, window_spec, pl.BlockSpec((1, LANES), lambda r, *_: (0, 0))],
            scratch_shapes=[pltpu.VMEM((slot_count, n + 16, n), F32)],
        ),
        name="extract",
    )(edge_colour, jnp.transpose(patch_offsets, (0, 1, 3, 2)), patch_live, node_ids, strips)
    sums = pl.pallas_call(
        functools.partial(stitch, half, rounds),
        out_shape=jax.ShapeDtypeStruct((4, NODE_DEV), F32),
        in_specs=[anywhere] * 2 + [whole] * 5,
        out_specs=whole,
        scratch_shapes=[
            pltpu.VMEM(windows, BF16),
            pltpu.VMEM((groups, GROUP, 2, n, n), F32),
            pltpu.VMEM(windows, BF16),
            pltpu.VMEM((rounds, 1, LANES), F32),
            pltpu.VMEM((4, LANES), F32),
            pltpu.VMEM((devices, 4, LANES), F32),
            sem(()),
            sem((groups,)),
            sem((groups,)),
            sem((rounds,)),
            sem((rounds,)),
            sem((devices,)),
            sem((devices,)),
            pltpu.SemaphoreType.REGULAR((devices.bit_length() - 1,)),
        ],
        compiler_params=pltpu.CompilerParams(collective_id=0, has_side_effects=True),
        name="stitch",
    )(kept, sent, line, *(jnp.asarray(t) for t in tables()))
    return sums[0:2] + sums[2:4]


def solution(mesh):
    placed = (
        P(("tiles", "grp"), None, None),
        P(("tiles", "grp"), None),
        P(("tiles", "grp"), None, None, None),
        P(("tiles", "grp"), None),
        P(("tiles", "grp"), None, None),
    )
    return jax.shard_map(
        on_device, mesh=mesh, in_specs=placed, out_specs=P(None, ("tiles", "grp")), check_vma=False
    )
```

```python
import functools
import math

import jax
import jax.numpy as jnp
import numpy as np
from jax import lax
from jax.experimental import pallas as pl
from jax.experimental.pallas import tpu as pltpu
from jax.sharding import PartitionSpec as P

PATCH = 128
NODE_DEV = 128
LANES = 128
PACK = 4
GROUP = 4

F32 = jnp.float32
BF16 = jnp.bfloat16
VMEM = pltpu.MemorySpace.VMEM
SMEM = pltpu.MemorySpace.SMEM


def split_np(x):
    hi = np.asarray(x, np.float32).astype(BF16)
    lo = (np.asarray(x, np.float64) - hi.astype(np.float64)).astype(np.float32).astype(BF16)
    return hi, lo


def tables():
    n = PATCH
    j = np.arange(n)
    angle = 2.0 * math.pi / n * ((j[:, None] * j[None, :]) % n)
    c, s = np.cos(angle), np.sin(angle)
    chi, clo = split_np(np.concatenate([c, s], axis=1))
    col = np.concatenate([chi, clo], axis=0)
    rhi, rlo = split_np(np.block([[c, -s], [s, c]]))
    row = np.concatenate([rhi, rlo, rhi], axis=1)
    ihi, ilo = split_np(np.concatenate([c, s], axis=1))
    inv_row = np.concatenate([ihi, ilo, ihi], axis=1)
    weight = np.where((j == 0) | (j == n // 2), 1.0, 2.0)[:, None]
    packed = np.where(j[:, None] <= n // 2, weight * c, -2.0 * s) / float(n * n)
    vhi, vlo = split_np(packed)
    inv_col = np.concatenate([vhi, vlo, vhi], axis=0)
    return col, row, inv_row, inv_col


def split(x):
    hi = x.astype(BF16)
    return hi, (x - hi.astype(F32)).astype(BF16)


def dot(a, b):
    return jnp.dot(a, b, preferred_element_type=F32)


def extract(half, colour_ref, offset_ref, live_ref, ids_ref, strips_ref, kept_ref, sent_ref, line_ref, blocks, tmp_ref, sems):
    n = PATCH
    slots = 2 * half
    rounds, height, width = strips_ref.shape
    parts = half // GROUP
    tile = lax.axis_index("tiles")
    last = lax.axis_size("tiles") // 2
    places = []
    for which in (1, 0):
        for r in range(rounds):
            side = (tile // (1 if r == 0 else last)) % 2
            for j in range(half):
                k = ((side + which) % 2) * half + j
                row, column = offset_ref[0, r, 0, k], offset_ref[0, r, 1, k]
                left = jnp.minimum(lax.div(column, LANES), width // LANES - 2) * LANES
                upper = jnp.minimum(lax.div(row, 16), (height - n) // 16 - 1) * 16
                i = len(places)
                copy = pltpu.make_async_copy(
                    strips_ref.at[
                        colour_ref[0, r],
                        pl.ds(pl.multiple_of(upper, 16), n + 16),
                        pl.ds(pl.multiple_of(left, LANES), 2 * LANES),
                    ],
                    blocks.at[i],
                    sems.at[i],
                )
                copy.start()
                shift = lax.rem(2 * LANES - (column - left), 2 * LANES)
                ref = sent_ref if which else kept_ref
                places.append((copy, shift, row - upper, ref, r * parts + j // GROUP, j % GROUP))
    for start in range(0, len(places), GROUP):
        for i in range(start, start + GROUP):
            copy, shift = places[i][:2]
            copy.wait()
            tmp_ref[i] = pltpu.roll(blocks[i].astype(F32), shift, 1)[:, :n]
        for i in range(start, start + GROUP):
            _, _, ahead, ref, g, p = places[i]
            ref[g, p] = tmp_ref[i, pl.ds(ahead, n), :].astype(BF16)
    lane = lax.broadcasted_iota(jnp.int32, (1, LANES), 1)
    ids = jnp.zeros((1, LANES), jnp.int32)
    for r in range(live_ref.shape[1]):
        for k in range(slots):
            node = jnp.where(k < live_ref[0, r], ids_ref[0, r, k], -1)
            ids = jnp.where(lane == r * slots + k, node, ids)
    line_ref[...] = ids.astype(F32)


def row_place(column, base):
    count = column.shape[0]
    lane = lax.broadcasted_iota(jnp.int32, (count, LANES), 1)
    sub = lax.broadcasted_iota(jnp.int32, (count, LANES), 0)
    return jnp.sum(jnp.where(lane == sub + base, column, 0.0), axis=0, keepdims=True)


def spectra(windows, col, row):
    n = PATCH
    x = jnp.concatenate(windows, axis=0)
    hi, lo = split(dot(jnp.concatenate([x, x], axis=1), col))

    def stack(v):
        return jnp.concatenate(
            [
                jnp.concatenate([v[:n, :n], v[n:, :n]], axis=1),
                jnp.concatenate([v[:n, n:], v[n:, n:]], axis=1),
            ],
            axis=0,
        )

    hi, lo = stack(hi), stack(lo)
    f = dot(row, jnp.concatenate([hi, hi, lo], axis=0))
    return [(f[:n, :n], f[n:, :n]), (f[:n, n:], f[n:, n:])]


def correlate(first, second, inv_row, inv_col):
    n = PATCH
    count = len(first)
    lane = lax.broadcasted_iota(jnp.int32, (n, n), 1)
    low = lane <= n // 2
    crosses = []
    mag_sums = []
    for (r1, i1), (r2, i2) in zip(first, second):
        cross_r = r1 * r2 + i1 * i2
        cross_i = r1 * i2 - i1 * r2
        mag = jnp.sqrt(cross_r * cross_r + cross_i * cross_i)
        crosses.append((cross_r, cross_i, mag))
        mag_sums.append(jnp.sum(mag, axis=0, keepdims=True))
    mean = jnp.sum(jnp.concatenate(mag_sums, axis=0), axis=1, keepdims=True) / float(n * n)
    extra = 0.1 * mean + 1e-06
    surfaces = []
    packed = []
    sums = []
    for p in range(count):
        cross_r, cross_i, mag = crosses[p]
        inverse = 1.0 / (mag + extra[p : p + 1])
        g_r = cross_r * inverse
        g_i = cross_i * inverse
        packed.append(
            split(jnp.concatenate([jnp.where(low, g_r, g_i), jnp.where(low, -g_i, g_r)], axis=0))
        )
    surfaces_wide = []
    for p in range(0, count, 2):
        hi = jnp.concatenate([packed[p][0], packed[p + 1][0]], axis=1)
        lo = jnp.concatenate([packed[p][1], packed[p + 1][1]], axis=1)
        b = dot(inv_row, jnp.concatenate([hi, hi, lo], axis=0))
        bhi, blo = split(jnp.concatenate([b[:, :n], b[:, n:]], axis=0))
        wide = dot(jnp.concatenate([bhi, bhi, blo], axis=1), inv_col)
        surfaces_wide += [wide[:n], wide[n:]]
    for surface in surfaces_wide:
        surfaces.append(surface)
        sums.append(jnp.sum(surface, axis=0, keepdims=True))
    centre = jnp.sum(jnp.concatenate(sums, axis=0), axis=1, keepdims=True) / float(n * n)
    squares = []
    tops = []
    for p in range(count):
        deviation = surfaces[p] - centre[p : p + 1]
        squares.append(jnp.sum(deviation * deviation, axis=0, keepdims=True))
        tops.append(jnp.max(surfaces[p], axis=0, keepdims=True))
    variance = jnp.sum(jnp.concatenate(squares, axis=0), axis=1, keepdims=True) / float(n * n)
    top = jnp.max(jnp.concatenate(tops, axis=0), axis=1, keepdims=True)
    scale = 2.0 / jnp.sqrt(variance + 1e-06)
    sub = lax.broadcasted_iota(jnp.int32, (n, n), 0)
    sub_coord = ((sub + n // 2) % n - n // 2).astype(F32)
    columns = []
    rows = []
    edges = []
    for p in range(count):
        e = jnp.exp((surfaces[p] - top[p : p + 1]) * scale[p : p + 1])
        columns.append(jnp.sum(e, axis=0, keepdims=True))
        rows.append(jnp.sum(e * sub_coord, axis=0, keepdims=True))
        edges.append(e[n // 2 : n // 2 + 1, :])
    columns = jnp.concatenate(columns, axis=0)
    rows = jnp.concatenate(rows, axis=0)
    edges = jnp.concatenate(edges, axis=0)
    lane = lax.broadcasted_iota(jnp.int32, (count, n), 1)
    lane_coord = ((lane + n // 2) % n - n // 2).astype(F32)

    def total(v):
        return jnp.sum(v, axis=1, keepdims=True)

    unit = float(n // 8)
    norm = 1.0 / total(columns)
    row_shift = total(rows) * norm / unit
    col_shift = total(columns * lane_coord) * norm / unit
    row_edge = total(edges) * norm * (float(n) / unit)
    col_edge = total(jnp.where(lane == n // 2, columns, 0.0)) * norm * (float(n) / unit)
    return row_shift, col_shift, -row_shift - row_edge, -col_shift - col_edge


MESH = pl.DeviceIdType.MESH


def stitch(
    half,
    rounds,
    kept_ref,
    sent,
    line,
    col_ref,
    row_ref,
    inv_row_ref,
    inv_col_ref,
    out_ref,
    kept,
    firsts,
    arrived,
    lines,
    tile_out,
    tiles,
    kept_sem,
    window_send,
    window_recv,
    line_send,
    line_recv,
    tile_send,
    tile_recv,
    hello,
):
    n = PATCH
    slots = 2 * half
    parts = half // GROUP
    groups = lax.axis_size("grp")
    tile_count = lax.axis_size("tiles")
    devices = tile_count * groups
    tile_index = lax.axis_index("tiles")
    me = tile_index * groups + lax.axis_index("grp")
    strides = [1] + [tile_count // 2] * (rounds - 1)
    sides = [(tile_index // s) % 2 for s in strides]
    partners = [tile_index + s * (1 - 2 * side) for s, side in zip(strides, sides)]

    load = pltpu.make_async_copy(kept_ref, kept, kept_sem)
    load.start()
    barrier = pltpu.get_barrier_semaphore()

    def device(d):
        return (d // groups, d % groups)

    neighbours = []
    stride = 1
    while stride < tile_count:
        bit = (tile_index // stride) % 2
        neighbours.append((tile_index + stride * (1 - 2 * bit), lax.axis_index("grp")))
        stride *= 2
    stride = 1
    while stride < groups:
        bit = (lax.axis_index("grp") // stride) % 2
        neighbours.append((tile_index, lax.axis_index("grp") + stride * (1 - 2 * bit)))
        stride *= 2
    stages = len(neighbours)
    for at in neighbours:
        pl.semaphore_signal(barrier, inc=1, device_id=at, device_id_type=MESH)

    def neighbour(stage):
        tile, group = neighbours[0]
        for i in range(1, stages):
            tile = jnp.where(stage == i, neighbours[i][0], tile)
            group = jnp.where(stage == i, neighbours[i][1], group)
        return tile, group

    def hail(stage):
        pl.semaphore_signal(
            hello.at[stage], inc=1, device_id=neighbour(stage), device_id_type=MESH
        )

    load.wait()

    def prepare(g, carry):
        for p in range(0, GROUP, 2):
            pair = spectra([kept[g, p], kept[g, p + 1]], col_ref[...], row_ref[...])
            for q in range(2):
                for c in range(2):
                    firsts[g, p + q, c] = pair[q][c]
        return carry

    lax.fori_loop(0, 1, prepare, 0)
    pl.semaphore_wait(barrier, stages)

    def window_copy(r, part):
        g = r * parts + part
        return pltpu.make_async_remote_copy(
            src_ref=sent.at[g],
            dst_ref=arrived.at[g],
            send_sem=window_send.at[g],
            recv_sem=window_recv.at[g],
            device_id=(partners[r], lax.axis_index("grp")),
            device_id_type=MESH,
        )

    def line_copy(r):
        return pltpu.make_async_remote_copy(
            src_ref=line,
            dst_ref=lines.at[r],
            send_sem=line_send.at[r],
            recv_sem=line_recv.at[r],
            device_id=(partners[r], lax.axis_index("grp")),
            device_id_type=MESH,
        )

    for part in range(parts):
        for r in range(rounds):
            window_copy(r, part).start()
    for r in range(rounds):
        line_copy(r).start()

    early = stages - rounds * parts
    for i in range(early):
        hail(i)
        if i == early - 1:
            lax.fori_loop(1, rounds * parts, prepare, 0)
        pl.semaphore_wait(hello.at[i], 1)

    def work(g, carry):
        r = g // parts
        hail(early + g)
        pltpu.make_async_remote_copy(
            src_ref=sent.at[g],
            dst_ref=arrived.at[g],
            send_sem=window_send.at[g],
            recv_sem=window_recv.at[g],
            device_id=(partners[0], lax.axis_index("grp")),
            device_id_type=MESH,
        ).wait_recv()
        side = sides[0]
        for i in range(1, rounds):
            side = jnp.where(r == i, sides[i], side)
        seconds = []
        for p in range(0, GROUP, 2):
            seconds += spectra([arrived[g, p], arrived[g, p + 1]], col_ref[...], row_ref[...])
        a, b, c, d = correlate(
            [(firsts[g, p, 0], firsts[g, p, 1]) for p in range(GROUP)],
            seconds,
            inv_row_ref[...],
            inv_col_ref[...],
        )
        base = r * slots + (g % parts) * GROUP
        own = base + side * half
        other = base + (1 - side) * half
        row_line, col_line = carry
        pl.semaphore_wait(hello.at[early + g], 1)
        return (
            row_line + row_place(a, own) + row_place(c, other),
            col_line + row_place(b, own) + row_place(d, other),
        )

    zero = jnp.zeros((1, LANES), F32)
    row_line, col_line = lax.fori_loop(0, rounds * parts, work, (zero, zero))

    lane = lax.broadcasted_iota(jnp.int32, (1, LANES), 1)
    ids = line[...]
    id_line = zero
    for r in range(rounds):
        line_copy(r).wait()
        theirs = pltpu.roll(lines[r], jnp.where(sides[r] == 0, half, LANES - half), 1)
        in_round = (lane >= r * slots) & (lane < (r + 1) * slots)
        mine = (lane // half) % 2 == sides[r]
        id_line = id_line + jnp.where(in_round, jnp.where(mine, ids, theirs), 0.0)
    tile = jnp.concatenate([row_line, col_line, id_line, zero], axis=0)
    tile = pltpu.roll(tile, (me % PACK) * (LANES // PACK), 1)
    tile_out[...] = tile
    tiles[me] = tile

    def tile_copy(i, slot):
        return pltpu.make_async_remote_copy(
            src_ref=tile_out,
            dst_ref=tiles.at[slot],
            send_sem=tile_send.at[i],
            recv_sem=tile_recv.at[slot],
            device_id=device((me + i) % devices),
            device_id_type=MESH,
        )

    def start(i, carry):
        tile_copy(i, me).start()
        return carry

    def receive(i, carry):
        tile_copy(i, (me + i) % devices).wait_recv()
        return carry

    def drain(i, carry):
        tile_copy(i, me).wait_send()
        return carry

    lax.fori_loop(1, devices, start, 0)
    for part in range(parts):
        for r in range(rounds):
            window_copy(r, part).wait_send()
    lax.fori_loop(1, devices, receive, 0)

    node = lax.broadcasted_iota(jnp.int32, (NODE_DEV, LANES), 0).astype(F32)
    first_node = (me * NODE_DEV).astype(F32)
    onehots = []
    values = []
    for g in range(devices // PACK):
        tile = tiles[g * PACK]
        for i in range(1, PACK):
            tile = tile + tiles[g * PACK + i]
        onehots.append(jnp.where(tile[2:3] - first_node == node, 1.0, 0.0).astype(BF16))
        hi = tile.astype(BF16).astype(F32)
        rest = tile - hi
        mid = rest.astype(BF16).astype(F32)
        values.append(jnp.concatenate([hi, mid, rest - mid, jnp.zeros_like(hi)], axis=0).astype(BF16))
    result = lax.dot_general(
        jnp.concatenate(values, axis=1),
        jnp.concatenate(onehots, axis=1),
        (((1,), (1,)), ((), ())),
        preferred_element_type=F32,
    )
    out_ref[0:2] = result[0:2]
    out_ref[2:4] = result[4:6] + result[8:10]
    lax.fori_loop(1, devices, drain, 0)


def on_device(strips, edge_colour, patch_offsets, patch_live, node_ids):
    rounds, height, width = strips.shape
    n = PATCH
    slot_count = patch_offsets.shape[2]
    half = slot_count // 2
    parts = half // GROUP
    groups = rounds * parts
    devices = lax.axis_size("tiles") * lax.axis_size("grp")
    whole = pl.BlockSpec(memory_space=VMEM)
    anywhere = pl.BlockSpec(memory_space=pl.ANY)
    sem = pltpu.SemaphoreType.DMA
    windows = (groups, GROUP, n, n)
    window_spec = pl.BlockSpec((parts, GROUP, n, n), lambda r, *_: (r, 0, 0, 0))
    kept, sent, line = pl.pallas_call(
        functools.partial(extract, half),
        out_shape=[jax.ShapeDtypeStruct(windows, BF16)] * 2 + [jax.ShapeDtypeStruct((1, LANES), F32)],
        in_specs=[pl.BlockSpec(memory_space=SMEM)] * 4 + [anywhere],
        out_specs=[whole] * 3,
        scratch_shapes=[
            pltpu.VMEM((rounds * slot_count, n + 16, 2 * LANES), BF16),
            pltpu.VMEM((rounds * slot_count, n + 16, n), F32),
            sem((rounds * slot_count,)),
        ],
        name="extract",
    )(edge_colour, jnp.transpose(patch_offsets, (0, 1, 3, 2)), patch_live, node_ids, strips)
    sums = pl.pallas_call(
        functools.partial(stitch, half, rounds),
        out_shape=jax.ShapeDtypeStruct((4, NODE_DEV), F32),
        in_specs=[anywhere] * 2 + [whole] * 5,
        out_specs=whole,
        scratch_shapes=[
            pltpu.VMEM(windows, BF16),
            pltpu.VMEM((groups, GROUP, 2, n, n), F32),
            pltpu.VMEM(windows, BF16),
            pltpu.VMEM((rounds, 1, LANES), F32),
            pltpu.VMEM((4, LANES), F32),
            pltpu.VMEM((devices, 4, LANES), F32),
            sem(()),
            sem((groups,)),
            sem((groups,)),
            sem((rounds,)),
            sem((rounds,)),
            sem((devices,)),
            sem((devices,)),
            pltpu.SemaphoreType.REGULAR((devices.bit_length() - 1,)),
        ],
        compiler_params=pltpu.CompilerParams(collective_id=0, has_side_effects=True),
        name="stitch",
    )(kept, sent, line, *(jnp.asarray(t) for t in tables()))
    return sums[0:2] + sums[2:4]


def solution(mesh):
    placed = (
        P(("tiles", "grp"), None, None),
        P(("tiles", "grp"), None),
        P(("tiles", "grp"), None, None, None),
        P(("tiles", "grp"), None),
        P(("tiles", "grp"), None, None),
    )
    return jax.shard_map(
        on_device, mesh=mesh, in_specs=placed, out_specs=P(None, ("tiles", "grp")), check_vma=False
    )
```

```python
import functools
import math

import jax
import jax.numpy as jnp
import numpy as np
from jax import lax
from jax.experimental import pallas as pl
from jax.experimental.pallas import tpu as pltpu
from jax.sharding import PartitionSpec as P

PATCH = 128
NODE_DEV = 128
LANES = 128
PACK = 4
GROUP = 4

F32 = jnp.float32
BF16 = jnp.bfloat16
VMEM = pltpu.MemorySpace.VMEM
SMEM = pltpu.MemorySpace.SMEM


def split_np(x):
    hi = np.asarray(x, np.float32).astype(BF16)
    lo = (np.asarray(x, np.float64) - hi.astype(np.float64)).astype(np.float32).astype(BF16)
    return hi, lo


def tables():
    n = PATCH
    j = np.arange(n)
    angle = 2.0 * math.pi / n * ((j[:, None] * j[None, :]) % n)
    c, s = np.cos(angle), np.sin(angle)
    chi, clo = split_np(np.concatenate([c, s], axis=1))
    col = np.concatenate([chi, clo], axis=0)
    rhi, rlo = split_np(np.block([[c, -s], [s, c]]))
    row = np.concatenate([rhi, rlo, rhi], axis=1)
    ihi, ilo = split_np(np.concatenate([c, s], axis=1))
    inv_row = np.concatenate([ihi, ilo, ihi], axis=1)
    weight = np.where((j == 0) | (j == n // 2), 1.0, 2.0)[:, None]
    packed = np.where(j[:, None] <= n // 2, weight * c, -2.0 * s) / float(n * n)
    vhi, vlo = split_np(packed)
    inv_col = np.concatenate([vhi, vlo, vhi], axis=0)
    return col, row, inv_row, inv_col


def split(x):
    hi = x.astype(BF16)
    return hi, (x - hi.astype(F32)).astype(BF16)


def dot(a, b):
    return jnp.dot(a, b, preferred_element_type=F32)


def extract(half, colour_ref, offset_ref, live_ref, ids_ref, strip_ref, kept_ref, sent_ref, line_ref, tmp_ref):
    n = PATCH
    slots = 2 * half
    rnd = pl.program_id(0)
    tile = lax.axis_index("tiles")
    side = jnp.where(rnd == 0, tile % 2, (tile // (lax.axis_size("tiles") // 2)) % 2)
    height, width = strip_ref.shape[1], strip_ref.shape[2]
    rows = []
    for j in range(slots):
        k = (side * half + half + j) % slots
        row, column = offset_ref[0, rnd, 0, k], offset_ref[0, rnd, 1, k]
        left = jnp.minimum(lax.div(column, LANES), width // LANES - 2) * LANES
        upper = jnp.minimum(lax.div(row, 16), (height - n) // 16 - 1) * 16
        block = strip_ref[
            0, pl.ds(pl.multiple_of(upper, 16), n + 16), pl.ds(pl.multiple_of(left, LANES), 2 * LANES)
        ].astype(F32)
        shift = lax.rem(2 * LANES - (column - left), 2 * LANES)
        tmp_ref[j] = pltpu.roll(block, shift, 1)[:, :n]
        rows.append(row - upper)
    for j in range(slots):
        window = tmp_ref[j, pl.ds(rows[j], n), :].astype(BF16)
        ref = sent_ref if j < half else kept_ref
        ref[j % half // GROUP, j % GROUP] = window
    lane = lax.broadcasted_iota(jnp.int32, (1, LANES), 1)
    ids = jnp.zeros((1, LANES), jnp.int32)
    for r in range(live_ref.shape[1]):
        for k in range(slots):
            node = jnp.where(k < live_ref[0, r], ids_ref[0, r, k], -1)
            ids = jnp.where(lane == r * slots + k, node, ids)
    line_ref[...] = ids.astype(F32)


def row_place(column, base):
    count = column.shape[0]
    lane = lax.broadcasted_iota(jnp.int32, (count, LANES), 1)
    sub = lax.broadcasted_iota(jnp.int32, (count, LANES), 0)
    return jnp.sum(jnp.where(lane == sub + base, column, 0.0), axis=0, keepdims=True)


def spectra(windows, col, row):
    n = PATCH
    x = jnp.concatenate(windows, axis=0)
    hi, lo = split(dot(jnp.concatenate([x, x], axis=1), col))

    def stack(v):
        return jnp.concatenate(
            [
                jnp.concatenate([v[:n, :n], v[n:, :n]], axis=1),
                jnp.concatenate([v[:n, n:], v[n:, n:]], axis=1),
            ],
            axis=0,
        )

    hi, lo = stack(hi), stack(lo)
    f = dot(row, jnp.concatenate([hi, hi, lo], axis=0))
    return [(f[:n, :n], f[n:, :n]), (f[:n, n:], f[n:, n:])]


def correlate(first, second, inv_row, inv_col):
    n = PATCH
    count = len(first)
    lane = lax.broadcasted_iota(jnp.int32, (n, n), 1)
    low = lane <= n // 2
    crosses = []
    mag_sums = []
    for (r1, i1), (r2, i2) in zip(first, second):
        cross_r = r1 * r2 + i1 * i2
        cross_i = r1 * i2 - i1 * r2
        mag = jnp.sqrt(cross_r * cross_r + cross_i * cross_i)
        crosses.append((cross_r, cross_i, mag))
        mag_sums.append(jnp.sum(mag, axis=0, keepdims=True))
    mean = jnp.sum(jnp.concatenate(mag_sums, axis=0), axis=1, keepdims=True) / float(n * n)
    extra = 0.1 * mean + 1e-06
    surfaces = []
    packed = []
    sums = []
    for p in range(count):
        cross_r, cross_i, mag = crosses[p]
        inverse = 1.0 / (mag + extra[p : p + 1])
        g_r = cross_r * inverse
        g_i = cross_i * inverse
        packed.append(
            split(jnp.concatenate([jnp.where(low, g_r, g_i), jnp.where(low, -g_i, g_r)], axis=0))
        )
    surfaces_wide = []
    for p in range(0, count, 2):
        hi = jnp.concatenate([packed[p][0], packed[p + 1][0]], axis=1)
        lo = jnp.concatenate([packed[p][1], packed[p + 1][1]], axis=1)
        b = dot(inv_row, jnp.concatenate([hi, hi, lo], axis=0))
        bhi, blo = split(jnp.concatenate([b[:, :n], b[:, n:]], axis=0))
        wide = dot(jnp.concatenate([bhi, bhi, blo], axis=1), inv_col)
        surfaces_wide += [wide[:n], wide[n:]]
    for surface in surfaces_wide:
        surfaces.append(surface)
        sums.append(jnp.sum(surface, axis=0, keepdims=True))
    centre = jnp.sum(jnp.concatenate(sums, axis=0), axis=1, keepdims=True) / float(n * n)
    squares = []
    tops = []
    for p in range(count):
        deviation = surfaces[p] - centre[p : p + 1]
        squares.append(jnp.sum(deviation * deviation, axis=0, keepdims=True))
        tops.append(jnp.max(surfaces[p], axis=0, keepdims=True))
    variance = jnp.sum(jnp.concatenate(squares, axis=0), axis=1, keepdims=True) / float(n * n)
    top = jnp.max(jnp.concatenate(tops, axis=0), axis=1, keepdims=True)
    scale = 2.0 / jnp.sqrt(variance + 1e-06)
    sub = lax.broadcasted_iota(jnp.int32, (n, n), 0)
    sub_coord = ((sub + n // 2) % n - n // 2).astype(F32)
    columns = []
    rows = []
    edges = []
    for p in range(count):
        e = jnp.exp((surfaces[p] - top[p : p + 1]) * scale[p : p + 1])
        columns.append(jnp.sum(e, axis=0, keepdims=True))
        rows.append(jnp.sum(e * sub_coord, axis=0, keepdims=True))
        edges.append(e[n // 2 : n // 2 + 1, :])
    columns = jnp.concatenate(columns, axis=0)
    rows = jnp.concatenate(rows, axis=0)
    edges = jnp.concatenate(edges, axis=0)
    lane = lax.broadcasted_iota(jnp.int32, (count, n), 1)
    lane_coord = ((lane + n // 2) % n - n // 2).astype(F32)

    def total(v):
        return jnp.sum(v, axis=1, keepdims=True)

    unit = float(n // 8)
    norm = 1.0 / total(columns)
    row_shift = total(rows) * norm / unit
    col_shift = total(columns * lane_coord) * norm / unit
    row_edge = total(edges) * norm * (float(n) / unit)
    col_edge = total(jnp.where(lane == n // 2, columns, 0.0)) * norm * (float(n) / unit)
    return row_shift, col_shift, -row_shift - row_edge, -col_shift - col_edge


MESH = pl.DeviceIdType.MESH


def stitch(
    half,
    rounds,
    kept_ref,
    sent,
    line,
    col_ref,
    row_ref,
    inv_row_ref,
    inv_col_ref,
    out_ref,
    kept,
    firsts,
    arrived,
    lines,
    tile_out,
    tiles,
    kept_sem,
    window_send,
    window_recv,
    line_send,
    line_recv,
    tile_send,
    tile_recv,
    hello,
):
    n = PATCH
    slots = 2 * half
    parts = half // GROUP
    groups = lax.axis_size("grp")
    tile_count = lax.axis_size("tiles")
    devices = tile_count * groups
    tile_index = lax.axis_index("tiles")
    me = tile_index * groups + lax.axis_index("grp")
    strides = [1] + [tile_count // 2] * (rounds - 1)
    sides = [(tile_index // s) % 2 for s in strides]
    partners = [tile_index + s * (1 - 2 * side) for s, side in zip(strides, sides)]

    load = pltpu.make_async_copy(kept_ref, kept, kept_sem)
    load.start()
    barrier = pltpu.get_barrier_semaphore()

    def device(d):
        return (d // groups, d % groups)

    neighbours = []
    stride = 1
    while stride < tile_count:
        bit = (tile_index // stride) % 2
        neighbours.append((tile_index + stride * (1 - 2 * bit), lax.axis_index("grp")))
        stride *= 2
    stride = 1
    while stride < groups:
        bit = (lax.axis_index("grp") // stride) % 2
        neighbours.append((tile_index, lax.axis_index("grp") + stride * (1 - 2 * bit)))
        stride *= 2
    stages = len(neighbours)
    for at in neighbours:
        pl.semaphore_signal(barrier, inc=1, device_id=at, device_id_type=MESH)

    def neighbour(stage):
        tile, group = neighbours[0]
        for i in range(1, stages):
            tile = jnp.where(stage == i, neighbours[i][0], tile)
            group = jnp.where(stage == i, neighbours[i][1], group)
        return tile, group

    def hail(stage):
        pl.semaphore_signal(
            hello.at[stage], inc=1, device_id=neighbour(stage), device_id_type=MESH
        )

    load.wait()

    def prepare(g, carry):
        for p in range(0, GROUP, 2):
            pair = spectra([kept[g, p], kept[g, p + 1]], col_ref[...], row_ref[...])
            for q in range(2):
                for c in range(2):
                    firsts[g, p + q, c] = pair[q][c]
        return carry

    lax.fori_loop(0, 1, prepare, 0)
    pl.semaphore_wait(barrier, stages)

    def window_copy(r, part):
        g = r * parts + part
        return pltpu.make_async_remote_copy(
            src_ref=sent.at[g],
            dst_ref=arrived.at[g],
            send_sem=window_send.at[g],
            recv_sem=window_recv.at[g],
            device_id=(partners[r], lax.axis_index("grp")),
            device_id_type=MESH,
        )

    def line_copy(r):
        return pltpu.make_async_remote_copy(
            src_ref=line,
            dst_ref=lines.at[r],
            send_sem=line_send.at[r],
            recv_sem=line_recv.at[r],
            device_id=(partners[r], lax.axis_index("grp")),
            device_id_type=MESH,
        )

    for part in range(parts):
        for r in reversed(range(rounds)):
            window_copy(r, part).start()
    for r in range(rounds):
        line_copy(r).start()

    early = stages - rounds * parts
    for i in range(early):
        hail(i)
        if i == early - 1:
            lax.fori_loop(1, rounds * parts, prepare, 0)
        pl.semaphore_wait(hello.at[i], 1)

    def work(g, carry):
        r = g // parts
        hail(early + g)
        pltpu.make_async_remote_copy(
            src_ref=sent.at[g],
            dst_ref=arrived.at[g],
            send_sem=window_send.at[g],
            recv_sem=window_recv.at[g],
            device_id=(partners[0], lax.axis_index("grp")),
            device_id_type=MESH,
        ).wait_recv()
        side = sides[0]
        for i in range(1, rounds):
            side = jnp.where(r == i, sides[i], side)
        seconds = []
        for p in range(0, GROUP, 2):
            seconds += spectra([arrived[g, p], arrived[g, p + 1]], col_ref[...], row_ref[...])
        a, b, c, d = correlate(
            [(firsts[g, p, 0], firsts[g, p, 1]) for p in range(GROUP)],
            seconds,
            inv_row_ref[...],
            inv_col_ref[...],
        )
        base = r * slots + (g % parts) * GROUP
        own = base + side * half
        other = base + (1 - side) * half
        row_line, col_line = carry
        pl.semaphore_wait(hello.at[early + g], 1)
        return (
            row_line + row_place(a, own) + row_place(c, other),
            col_line + row_place(b, own) + row_place(d, other),
        )

    zero = jnp.zeros((1, LANES), F32)
    row_line, col_line = lax.fori_loop(0, rounds * parts, work, (zero, zero))

    lane = lax.broadcasted_iota(jnp.int32, (1, LANES), 1)
    ids = line[...]
    id_line = zero
    for r in range(rounds):
        line_copy(r).wait()
        theirs = pltpu.roll(lines[r], jnp.where(sides[r] == 0, half, LANES - half), 1)
        in_round = (lane >= r * slots) & (lane < (r + 1) * slots)
        mine = (lane // half) % 2 == sides[r]
        id_line = id_line + jnp.where(in_round, jnp.where(mine, ids, theirs), 0.0)
    tile = jnp.concatenate([row_line, col_line, id_line, zero], axis=0)
    tile = pltpu.roll(tile, (me % PACK) * (LANES // PACK), 1)
    tile_out[...] = tile
    tiles[me] = tile

    def tile_copy(i, slot):
        return pltpu.make_async_remote_copy(
            src_ref=tile_out,
            dst_ref=tiles.at[slot],
            send_sem=tile_send.at[i],
            recv_sem=tile_recv.at[slot],
            device_id=device((me + i) % devices),
            device_id_type=MESH,
        )

    def start(i, carry):
        tile_copy(i, me).start()
        return carry

    def receive(i, carry):
        tile_copy(i, (me + i) % devices).wait_recv()
        return carry

    def drain(i, carry):
        tile_copy(i, me).wait_send()
        return carry

    lax.fori_loop(1, devices, start, 0)
    for part in range(parts):
        for r in range(rounds):
            window_copy(r, part).wait_send()
    lax.fori_loop(1, devices, receive, 0)

    node = lax.broadcasted_iota(jnp.int32, (NODE_DEV, LANES), 0).astype(F32)
    first_node = (me * NODE_DEV).astype(F32)
    onehots = []
    values = []
    for g in range(devices // PACK):
        tile = tiles[g * PACK]
        for i in range(1, PACK):
            tile = tile + tiles[g * PACK + i]
        onehots.append(jnp.where(tile[2:3] - first_node == node, 1.0, 0.0).astype(BF16))
        hi = tile.astype(BF16).astype(F32)
        rest = tile - hi
        mid = rest.astype(BF16).astype(F32)
        values.append(jnp.concatenate([hi, mid, rest - mid, jnp.zeros_like(hi)], axis=0).astype(BF16))
    result = lax.dot_general(
        jnp.concatenate(values, axis=1),
        jnp.concatenate(onehots, axis=1),
        (((1,), (1,)), ((), ())),
        preferred_element_type=F32,
    )
    out_ref[0:2] = result[0:2]
    out_ref[2:4] = result[4:6] + result[8:10]
    lax.fori_loop(1, devices, drain, 0)


def on_device(strips, edge_colour, patch_offsets, patch_live, node_ids):
    rounds, height, width = strips.shape
    n = PATCH
    slot_count = patch_offsets.shape[2]
    half = slot_count // 2
    parts = half // GROUP
    groups = rounds * parts
    devices = lax.axis_size("tiles") * lax.axis_size("grp")
    whole = pl.BlockSpec(memory_space=VMEM)
    anywhere = pl.BlockSpec(memory_space=pl.ANY)
    sem = pltpu.SemaphoreType.DMA
    windows = (groups, GROUP, n, n)
    window_spec = pl.BlockSpec((parts, GROUP, n, n), lambda r, *_: (r, 0, 0, 0))
    kept, sent, line = pl.pallas_call(
        functools.partial(extract, half),
        out_shape=[jax.ShapeDtypeStruct(windows, BF16)] * 2 + [jax.ShapeDtypeStruct((1, LANES), F32)],
        grid_spec=pltpu.PrefetchScalarGridSpec(
            num_scalar_prefetch=4,
            grid=(rounds,),
            in_specs=[pl.BlockSpec((1, height, width), lambda r, colour, *_: (colour[0, r], 0, 0))],
            out_specs=[window_spec, window_spec, pl.BlockSpec((1, LANES), lambda r, *_: (0, 0))],
            scratch_shapes=[pltpu.VMEM((slot_count, n + 16, n), F32)],
        ),
        name="extract",
    )(edge_colour, jnp.transpose(patch_offsets, (0, 1, 3, 2)), patch_live, node_ids, strips)
    sums = pl.pallas_call(
        functools.partial(stitch, half, rounds),
        out_shape=jax.ShapeDtypeStruct((4, NODE_DEV), F32),
        in_specs=[anywhere] * 2 + [whole] * 5,
        out_specs=whole,
        scratch_shapes=[
            pltpu.VMEM(windows, BF16),
            pltpu.VMEM((groups, GROUP, 2, n, n), F32),
            pltpu.VMEM(windows, BF16),
            pltpu.VMEM((rounds, 1, LANES), F32),
            pltpu.VMEM((4, LANES), F32),
            pltpu.VMEM((devices, 4, LANES), F32),
            sem(()),
            sem((groups,)),
            sem((groups,)),
            sem((rounds,)),
            sem((rounds,)),
            sem((devices,)),
            sem((devices,)),
            pltpu.SemaphoreType.REGULAR((devices.bit_length() - 1,)),
        ],
        compiler_params=pltpu.CompilerParams(collective_id=0, has_side_effects=True),
        name="stitch",
    )(kept, sent, line, *(jnp.asarray(t) for t in tables()))
    return sums[0:2] + sums[2:4]


def solution(mesh):
    placed = (
        P(("tiles", "grp"), None, None),
        P(("tiles", "grp"), None),
        P(("tiles", "grp"), None, None, None),
        P(("tiles", "grp"), None),
        P(("tiles", "grp"), None, None),
    )
    return jax.shard_map(
        on_device, mesh=mesh, in_specs=placed, out_specs=P(None, ("tiles", "grp")), check_vma=False
    )
```

```python
import functools
import math

import jax
import jax.numpy as jnp
import numpy as np
from jax import lax
from jax.experimental import pallas as pl
from jax.experimental.pallas import tpu as pltpu
from jax.sharding import PartitionSpec as P

PATCH = 128
NODE_DEV = 128
LANES = 128
PACK = 4
GROUP = 2

F32 = jnp.float32
BF16 = jnp.bfloat16
VMEM = pltpu.MemorySpace.VMEM
SMEM = pltpu.MemorySpace.SMEM


def split_np(x):
    hi = np.asarray(x, np.float32).astype(BF16)
    lo = (np.asarray(x, np.float64) - hi.astype(np.float64)).astype(np.float32).astype(BF16)
    return hi, lo


def tables():
    n = PATCH
    j = np.arange(n)
    angle = 2.0 * math.pi / n * ((j[:, None] * j[None, :]) % n)
    c, s = np.cos(angle), np.sin(angle)
    chi, clo = split_np(np.concatenate([c, s], axis=1))
    col = np.concatenate([chi, clo], axis=0)
    rhi, rlo = split_np(np.block([[c, -s], [s, c]]))
    row = np.concatenate([rhi, rlo, rhi], axis=1)
    ihi, ilo = split_np(np.concatenate([c, s], axis=1))
    inv_row = np.concatenate([ihi, ilo, ihi], axis=1)
    weight = np.where((j == 0) | (j == n // 2), 1.0, 2.0)[:, None]
    packed = np.where(j[:, None] <= n // 2, weight * c, -2.0 * s) / float(n * n)
    vhi, vlo = split_np(packed)
    inv_col = np.concatenate([vhi, vlo, vhi], axis=0)
    return col, row, inv_row, inv_col


def split(x):
    hi = x.astype(BF16)
    return hi, (x - hi.astype(F32)).astype(BF16)


def dot(a, b):
    return jnp.dot(a, b, preferred_element_type=F32)


def extract(half, colour_ref, offset_ref, live_ref, ids_ref, strip_ref, kept_ref, sent_ref, line_ref, tmp_ref):
    n = PATCH
    slots = 2 * half
    rnd = pl.program_id(0)
    tile = lax.axis_index("tiles")
    side = jnp.where(rnd == 0, tile % 2, (tile // (lax.axis_size("tiles") // 2)) % 2)
    height, width = strip_ref.shape[1], strip_ref.shape[2]
    rows = []
    for j in range(slots):
        k = (side * half + half + j) % slots
        row, column = offset_ref[0, rnd, 0, k], offset_ref[0, rnd, 1, k]
        left = jnp.minimum(lax.div(column, LANES), width // LANES - 2) * LANES
        upper = jnp.minimum(lax.div(row, 16), (height - n) // 16 - 1) * 16
        block = strip_ref[
            0, pl.ds(pl.multiple_of(upper, 16), n + 16), pl.ds(pl.multiple_of(left, LANES), 2 * LANES)
        ].astype(F32)
        shift = lax.rem(2 * LANES - (column - left), 2 * LANES)
        tmp_ref[j] = pltpu.roll(block, shift, 1)[:, :n]
        rows.append(row - upper)
    for j in range(slots):
        window = tmp_ref[j, pl.ds(rows[j], n), :].astype(BF16)
        ref = sent_ref if j < half else kept_ref
        ref[j % half // GROUP, j % GROUP] = window
    lane = lax.broadcasted_iota(jnp.int32, (1, LANES), 1)
    ids = jnp.zeros((1, LANES), jnp.int32)
    for r in range(live_ref.shape[1]):
        for k in range(slots):
            node = jnp.where(k < live_ref[0, r], ids_ref[0, r, k], -1)
            ids = jnp.where(lane == r * slots + k, node, ids)
    line_ref[...] = ids.astype(F32)


def row_place(column, base):
    count = column.shape[0]
    lane = lax.broadcasted_iota(jnp.int32, (count, LANES), 1)
    sub = lax.broadcasted_iota(jnp.int32, (count, LANES), 0)
    return jnp.sum(jnp.where(lane == sub + base, column, 0.0), axis=0, keepdims=True)


def spectra(windows, col, row):
    n = PATCH
    x = jnp.concatenate(windows, axis=0)
    hi, lo = split(dot(jnp.concatenate([x, x], axis=1), col))

    def stack(v):
        return jnp.concatenate(
            [
                jnp.concatenate([v[:n, :n], v[n:, :n]], axis=1),
                jnp.concatenate([v[:n, n:], v[n:, n:]], axis=1),
            ],
            axis=0,
        )

    hi, lo = stack(hi), stack(lo)
    f = dot(row, jnp.concatenate([hi, hi, lo], axis=0))
    return [(f[:n, :n], f[n:, :n]), (f[:n, n:], f[n:, n:])]


def correlate(first, second, inv_row, inv_col):
    n = PATCH
    count = len(first)
    lane = lax.broadcasted_iota(jnp.int32, (n, n), 1)
    low = lane <= n // 2
    crosses = []
    mag_sums = []
    for (r1, i1), (r2, i2) in zip(first, second):
        cross_r = r1 * r2 + i1 * i2
        cross_i = r1 * i2 - i1 * r2
        mag = jnp.sqrt(cross_r * cross_r + cross_i * cross_i)
        crosses.append((cross_r, cross_i, mag))
        mag_sums.append(jnp.sum(mag, axis=0, keepdims=True))
    mean = jnp.sum(jnp.concatenate(mag_sums, axis=0), axis=1, keepdims=True) / float(n * n)
    extra = 0.1 * mean + 1e-06
    surfaces = []
    packed = []
    sums = []
    for p in range(count):
        cross_r, cross_i, mag = crosses[p]
        inverse = 1.0 / (mag + extra[p : p + 1])
        g_r = cross_r * inverse
        g_i = cross_i * inverse
        packed.append(
            split(jnp.concatenate([jnp.where(low, g_r, g_i), jnp.where(low, -g_i, g_r)], axis=0))
        )
    surfaces_wide = []
    for p in range(0, count, 2):
        hi = jnp.concatenate([packed[p][0], packed[p + 1][0]], axis=1)
        lo = jnp.concatenate([packed[p][1], packed[p + 1][1]], axis=1)
        b = dot(inv_row, jnp.concatenate([hi, hi, lo], axis=0))
        bhi, blo = split(jnp.concatenate([b[:, :n], b[:, n:]], axis=0))
        wide = dot(jnp.concatenate([bhi, bhi, blo], axis=1), inv_col)
        surfaces_wide += [wide[:n], wide[n:]]
    for surface in surfaces_wide:
        surfaces.append(surface)
        sums.append(jnp.sum(surface, axis=0, keepdims=True))
    centre = jnp.sum(jnp.concatenate(sums, axis=0), axis=1, keepdims=True) / float(n * n)
    squares = []
    tops = []
    for p in range(count):
        deviation = surfaces[p] - centre[p : p + 1]
        squares.append(jnp.sum(deviation * deviation, axis=0, keepdims=True))
        tops.append(jnp.max(surfaces[p], axis=0, keepdims=True))
    variance = jnp.sum(jnp.concatenate(squares, axis=0), axis=1, keepdims=True) / float(n * n)
    top = jnp.max(jnp.concatenate(tops, axis=0), axis=1, keepdims=True)
    scale = 2.0 / jnp.sqrt(variance + 1e-06)
    sub = lax.broadcasted_iota(jnp.int32, (n, n), 0)
    sub_coord = ((sub + n // 2) % n - n // 2).astype(F32)
    columns = []
    rows = []
    edges = []
    for p in range(count):
        e = jnp.exp((surfaces[p] - top[p : p + 1]) * scale[p : p + 1])
        columns.append(jnp.sum(e, axis=0, keepdims=True))
        rows.append(jnp.sum(e * sub_coord, axis=0, keepdims=True))
        edges.append(e[n // 2 : n // 2 + 1, :])
    columns = jnp.concatenate(columns, axis=0)
    rows = jnp.concatenate(rows, axis=0)
    edges = jnp.concatenate(edges, axis=0)
    lane = lax.broadcasted_iota(jnp.int32, (count, n), 1)
    lane_coord = ((lane + n // 2) % n - n // 2).astype(F32)

    def total(v):
        return jnp.sum(v, axis=1, keepdims=True)

    unit = float(n // 8)
    norm = 1.0 / total(columns)
    row_shift = total(rows) * norm / unit
    col_shift = total(columns * lane_coord) * norm / unit
    row_edge = total(edges) * norm * (float(n) / unit)
    col_edge = total(jnp.where(lane == n // 2, columns, 0.0)) * norm * (float(n) / unit)
    return row_shift, col_shift, -row_shift - row_edge, -col_shift - col_edge


MESH = pl.DeviceIdType.MESH


def stitch(
    half,
    rounds,
    kept_ref,
    sent,
    line,
    col_ref,
    row_ref,
    inv_row_ref,
    inv_col_ref,
    out_ref,
    kept,
    firsts,
    arrived,
    lines,
    tile_out,
    tiles,
    kept_sem,
    window_send,
    window_recv,
    line_send,
    line_recv,
    tile_send,
    tile_recv,
    hello,
):
    n = PATCH
    slots = 2 * half
    parts = half // GROUP
    groups = lax.axis_size("grp")
    tile_count = lax.axis_size("tiles")
    devices = tile_count * groups
    tile_index = lax.axis_index("tiles")
    me = tile_index * groups + lax.axis_index("grp")
    strides = [1] + [tile_count // 2] * (rounds - 1)
    sides = [(tile_index // s) % 2 for s in strides]
    partners = [tile_index + s * (1 - 2 * side) for s, side in zip(strides, sides)]

    load = pltpu.make_async_copy(kept_ref, kept, kept_sem)
    load.start()
    barrier = pltpu.get_barrier_semaphore()

    def device(d):
        return (d // groups, d % groups)

    neighbours = []
    stride = 1
    while stride < tile_count:
        bit = (tile_index // stride) % 2
        neighbours.append((tile_index + stride * (1 - 2 * bit), lax.axis_index("grp")))
        stride *= 2
    stride = 1
    while stride < groups:
        bit = (lax.axis_index("grp") // stride) % 2
        neighbours.append((tile_index, lax.axis_index("grp") + stride * (1 - 2 * bit)))
        stride *= 2
    stages = len(neighbours)
    for at in neighbours:
        pl.semaphore_signal(barrier, inc=1, device_id=at, device_id_type=MESH)

    def neighbour(stage):
        tile, group = neighbours[0]
        for i in range(1, stages):
            tile = jnp.where(stage == i, neighbours[i][0], tile)
            group = jnp.where(stage == i, neighbours[i][1], group)
        return tile, group

    def hail(stage):
        pl.semaphore_signal(
            hello.at[stage], inc=1, device_id=neighbour(stage), device_id_type=MESH
        )

    load.wait()

    def prepare(g, carry):
        for p in range(0, GROUP, 2):
            pair = spectra([kept[g, p], kept[g, p + 1]], col_ref[...], row_ref[...])
            for q in range(2):
                for c in range(2):
                    firsts[g, p + q, c] = pair[q][c]
        return carry

    lax.fori_loop(0, 1, prepare, 0)
    pl.semaphore_wait(barrier, stages)

    def window_copy(r, part):
        g = r * parts + part
        return pltpu.make_async_remote_copy(
            src_ref=sent.at[g],
            dst_ref=arrived.at[g],
            send_sem=window_send.at[g],
            recv_sem=window_recv.at[g],
            device_id=(partners[r], lax.axis_index("grp")),
            device_id_type=MESH,
        )

    def line_copy(r):
        return pltpu.make_async_remote_copy(
            src_ref=line,
            dst_ref=lines.at[r],
            send_sem=line_send.at[r],
            recv_sem=line_recv.at[r],
            device_id=(partners[r], lax.axis_index("grp")),
            device_id_type=MESH,
        )

    for part in range(parts):
        for r in range(rounds):
            window_copy(r, part).start()
    for r in range(rounds):
        line_copy(r).start()

    early = stages - rounds * parts
    for i in range(early):
        hail(i)
        if i == early - 1:
            lax.fori_loop(1, rounds * parts, prepare, 0)
        pl.semaphore_wait(hello.at[i], 1)
    if early <= 0:
        lax.fori_loop(1, rounds * parts, prepare, 0)

    def work(g, carry):
        r = g // parts

        @pl.when(g + early >= 0)
        def _():
            hail(early + g)

        pltpu.make_async_remote_copy(
            src_ref=sent.at[g],
            dst_ref=arrived.at[g],
            send_sem=window_send.at[g],
            recv_sem=window_recv.at[g],
            device_id=(partners[0], lax.axis_index("grp")),
            device_id_type=MESH,
        ).wait_recv()
        side = sides[0]
        for i in range(1, rounds):
            side = jnp.where(r == i, sides[i], side)
        seconds = []
        for p in range(0, GROUP, 2):
            seconds += spectra([arrived[g, p], arrived[g, p + 1]], col_ref[...], row_ref[...])
        a, b, c, d = correlate(
            [(firsts[g, p, 0], firsts[g, p, 1]) for p in range(GROUP)],
            seconds,
            inv_row_ref[...],
            inv_col_ref[...],
        )
        base = r * slots + (g % parts) * GROUP
        own = base + side * half
        other = base + (1 - side) * half
        row_line, col_line = carry

        @pl.when(g + early >= 0)
        def _():
            pl.semaphore_wait(hello.at[early + g], 1)

        return (
            row_line + row_place(a, own) + row_place(c, other),
            col_line + row_place(b, own) + row_place(d, other),
        )

    zero = jnp.zeros((1, LANES), F32)
    row_line, col_line = lax.fori_loop(0, rounds * parts, work, (zero, zero))

    lane = lax.broadcasted_iota(jnp.int32, (1, LANES), 1)
    ids = line[...]
    id_line = zero
    for r in range(rounds):
        line_copy(r).wait()
        theirs = pltpu.roll(lines[r], jnp.where(sides[r] == 0, half, LANES - half), 1)
        in_round = (lane >= r * slots) & (lane < (r + 1) * slots)
        mine = (lane // half) % 2 == sides[r]
        id_line = id_line + jnp.where(in_round, jnp.where(mine, ids, theirs), 0.0)
    tile = jnp.concatenate([row_line, col_line, id_line, zero], axis=0)
    tile = pltpu.roll(tile, (me % PACK) * (LANES // PACK), 1)
    tile_out[...] = tile
    tiles[me] = tile

    def tile_copy(i, slot):
        return pltpu.make_async_remote_copy(
            src_ref=tile_out,
            dst_ref=tiles.at[slot],
            send_sem=tile_send.at[i],
            recv_sem=tile_recv.at[slot],
            device_id=device((me + i) % devices),
            device_id_type=MESH,
        )

    def start(i, carry):
        tile_copy(i, me).start()
        return carry

    def receive(i, carry):
        tile_copy(i, (me + i) % devices).wait_recv()
        return carry

    def drain(i, carry):
        tile_copy(i, me).wait_send()
        return carry

    lax.fori_loop(1, devices, start, 0)
    for part in range(parts):
        for r in range(rounds):
            window_copy(r, part).wait_send()
    lax.fori_loop(1, devices, receive, 0)

    node = lax.broadcasted_iota(jnp.int32, (NODE_DEV, LANES), 0).astype(F32)
    first_node = (me * NODE_DEV).astype(F32)
    onehots = []
    values = []
    for g in range(devices // PACK):
        tile = tiles[g * PACK]
        for i in range(1, PACK):
            tile = tile + tiles[g * PACK + i]
        onehots.append(jnp.where(tile[2:3] - first_node == node, 1.0, 0.0).astype(BF16))
        hi = tile.astype(BF16).astype(F32)
        rest = tile - hi
        mid = rest.astype(BF16).astype(F32)
        values.append(jnp.concatenate([hi, mid, rest - mid, jnp.zeros_like(hi)], axis=0).astype(BF16))
    result = lax.dot_general(
        jnp.concatenate(values, axis=1),
        jnp.concatenate(onehots, axis=1),
        (((1,), (1,)), ((), ())),
        preferred_element_type=F32,
    )
    out_ref[0:2] = result[0:2]
    out_ref[2:4] = result[4:6] + result[8:10]
    lax.fori_loop(1, devices, drain, 0)


def on_device(strips, edge_colour, patch_offsets, patch_live, node_ids):
    rounds, height, width = strips.shape
    n = PATCH
    slot_count = patch_offsets.shape[2]
    half = slot_count // 2
    parts = half // GROUP
    groups = rounds * parts
    devices = lax.axis_size("tiles") * lax.axis_size("grp")
    whole = pl.BlockSpec(memory_space=VMEM)
    anywhere = pl.BlockSpec(memory_space=pl.ANY)
    sem = pltpu.SemaphoreType.DMA
    windows = (groups, GROUP, n, n)
    window_spec = pl.BlockSpec((parts, GROUP, n, n), lambda r, *_: (r, 0, 0, 0))
    kept, sent, line = pl.pallas_call(
        functools.partial(extract, half),
        out_shape=[jax.ShapeDtypeStruct(windows, BF16)] * 2 + [jax.ShapeDtypeStruct((1, LANES), F32)],
        grid_spec=pltpu.PrefetchScalarGridSpec(
            num_scalar_prefetch=4,
            grid=(rounds,),
            in_specs=[pl.BlockSpec((1, height, width), lambda r, colour, *_: (colour[0, r], 0, 0))],
            out_specs=[window_spec, window_spec, pl.BlockSpec((1, LANES), lambda r, *_: (0, 0))],
            scratch_shapes=[pltpu.VMEM((slot_count, n + 16, n), F32)],
        ),
        name="extract",
    )(edge_colour, jnp.transpose(patch_offsets, (0, 1, 3, 2)), patch_live, node_ids, strips)
    sums = pl.pallas_call(
        functools.partial(stitch, half, rounds),
        out_shape=jax.ShapeDtypeStruct((4, NODE_DEV), F32),
        in_specs=[anywhere] * 2 + [whole] * 5,
        out_specs=whole,
        scratch_shapes=[
            pltpu.VMEM(windows, BF16),
            pltpu.VMEM((groups, GROUP, 2, n, n), F32),
            pltpu.VMEM(windows, BF16),
            pltpu.VMEM((rounds, 1, LANES), F32),
            pltpu.VMEM((4, LANES), F32),
            pltpu.VMEM((devices, 4, LANES), F32),
            sem(()),
            sem((groups,)),
            sem((groups,)),
            sem((rounds,)),
            sem((rounds,)),
            sem((devices,)),
            sem((devices,)),
            pltpu.SemaphoreType.REGULAR((devices.bit_length() - 1,)),
        ],
        compiler_params=pltpu.CompilerParams(collective_id=0, has_side_effects=True),
        name="stitch",
    )(kept, sent, line, *(jnp.asarray(t) for t in tables()))
    return sums[0:2] + sums[2:4]


def solution(mesh):
    placed = (
        P(("tiles", "grp"), None, None),
        P(("tiles", "grp"), None),
        P(("tiles", "grp"), None, None, None),
        P(("tiles", "grp"), None),
        P(("tiles", "grp"), None, None),
    )
    return jax.shard_map(
        on_device, mesh=mesh, in_specs=placed, out_specs=P(None, ("tiles", "grp")), check_vma=False
    )
```
